256 devices in a mesh: slab: 64 (over z, y, core), col: 4 (over x).
Axes of the slice: x: 4, y: 4, z: 8, core: 2. Of those that a mesh axis runs over, the one named last changes fastest.
Arguments:
- recycle_basis: float32 [16, 3, 128, 8, 256], P('col', None, 'slab'), may hold values from -400 to 400
- densities: float32 [128, 8, 256], P('slab'), may hold values from 0.2 to 1
- solid_mask: int32 [128, 8, 256], P('slab'), may hold values 0 or 1
- fixed_mask: int32 [128, 8, 256], P('slab'), may hold values 0 or 1
Outputs:
- ortho_basis: float32 [16, 3, 128, 8, 256], P('col', None, 'slab')
- new_recycle: float32 [16, 3, 128, 8, 256], P('col', None, 'slab')
- r_factor: float32 [16, 16], replicated
The draws below stay inside these ranges and needn't reach their ends.
Inputs may be any that keep to these rules, and one draw needn't show every extreme that they name: `solid_mask`: 1 marks a solid lattice voxel. `fixed_mask`: 1 marks a fixed node.
All inputs are finite; a program needn't handle non-finite values. No bound on the sum of `solid_mask` or of `fixed_mask` on one device may be relied on, other than what follows from the above.
Results may differ from the reference program's by a relative error of at most 0.0001.
Values sent between devices are 32-bit elements; how exact they have to be, the bound alone decides.
A program may use at most 64 MiB of HBM per device.

```python
import math
import jax
import jax.numpy as jnp
import numpy as np
from jax import lax

COLS = 16
NXS = 8
NYS = 256
NZ = 128
ROWS = 786432


def draw_recycle_basis(key, part):
    key_order, key_main = jax.random.split(key, 2)
    full_shape = (COLS, 3, NZ, NXS, NYS)
    ranking = jax.random.permutation(key_order, COLS).astype(jnp.float32)
    column_scale = (10.0 ** (ranking / (COLS - 1))).reshape(COLS, 1, 1, 1, 1)
    depth_index = lax.broadcasted_iota(jnp.float32, (1, 1, NZ, 1, 1), 2)
    depth_scale = 10.0 ** (depth_index / (NZ - 1))
    sample = jnp.clip(jax.random.normal(key_main, full_shape, jnp.float32), -4.0, 4.0)
    return sample * column_scale * depth_scale


def place_ends(entries, own_key, least, top_value):
    extent = entries.shape
    place = [jax.random.randint(jax.random.fold_in(own_key, axis), (), 0, extent[axis]) for axis in range(len(extent))]
    entries = entries.at[tuple(place)].set(least)
    longest = extent.index(max(extent))
    place[longest] = (place[longest] + 1) % extent[longest]
    return entries.at[tuple(place)].set(top_value)


def block_scale(rng, extent, cuts, least, top_value):
    def one(position, shards_of):
        steps = jax.random.uniform(jax.random.fold_in(jax.random.fold_in(rng, 6), position), (shards_of,), jnp.float32, least / len(cuts), top_value / len(cuts))
        return jnp.repeat(jnp.exp(steps), extent[position] // shards_of).reshape((-1,) + (1,) * (len(extent) - position - 1))

    gain = one(*cuts[0])
    for cut in cuts[1:]:
        gain = gain * one(*cut)
    return gain


def setup_inputs(seed: int = 0) -> dict:
    arg_keys = jax.random.split(jax.random.key(seed), 5)
    return {
        "recycle_basis": draw_recycle_basis(jax.random.fold_in(arg_keys[4], 71), 0),
        "densities": jnp.clip(jnp.exp(math.log(1.0) - 1.609438 * jax.random.uniform(arg_keys[1], (NZ, NXS, NYS), jnp.float32) ** block_scale(arg_keys[1], (NZ, NXS, NYS), ((0, 64),), -0.2, 0.2)), 0.2, 1.0),
        "solid_mask": place_ends((jax.random.randint(arg_keys[2], (NZ, NXS, NYS), 0, 4) < 3).astype(jnp.int32), jax.random.fold_in(arg_keys[2], 1), 0, 1),
        "fixed_mask": place_ends((jax.random.randint(arg_keys[3], (NZ, NXS, NYS), 0, 16) < 1).astype(jnp.int32), jax.random.fold_in(arg_keys[3], 1), 0, 1),
    }


void_stiffness = 0.001

def element_matrix():
    poisson = 0.3
    lame_first = poisson / ((1.0 + poisson) * (1.0 - 2.0 * poisson))
    shear_mod = 1.0 / (2.0 * (1.0 + poisson))
    elastic = np.zeros((6, 6))
    elastic[:3, :3] = lame_first
    for k in range(3):
        elastic[k, k] = lame_first + 2.0 * shear_mod
    for k in range(3, 6):
        elastic[k, k] = shear_mod
    points = [(1.0 - 1.0 / np.sqrt(3.0)) / 2.0, (1.0 + 1.0 / np.sqrt(3.0)) / 2.0]
    matrix = np.zeros((24, 24))
    for a in points:
        for b in points:
            for d in points:
                strain = np.zeros((6, 24))
                for c in range(8):
                    ox, oy, oz = (c % 2, c // 2 % 2, c // 4)
                    weight_x = a if ox else 1.0 - a
                    weight_y = b if oy else 1.0 - b
                    weight_z = d if oz else 1.0 - d
                    slope_x = (1.0 if ox else -1.0) * weight_y * weight_z
                    slope_y = (1.0 if oy else -1.0) * weight_x * weight_z
                    slope_z = (1.0 if oz else -1.0) * weight_x * weight_y
                    strain[0, 3 * c] = slope_x
                    strain[1, 3 * c + 1] = slope_y
                    strain[2, 3 * c + 2] = slope_z
                    strain[3, 3 * c] = slope_y
                    strain[3, 3 * c + 1] = slope_x
                    strain[4, 3 * c + 1] = slope_z
                    strain[4, 3 * c + 2] = slope_y
                    strain[5, 3 * c] = slope_z
                    strain[5, 3 * c + 2] = slope_x
                matrix = matrix + strain.T @ elastic @ strain / 8.0
    return matrix.reshape(8, 3, 8, 3)

def shift_ahead(values, along):
    count = values.shape[along]
    rest = lax.slice_in_dim(values, 1, count, axis=along)
    edge = jnp.zeros_like(lax.slice_in_dim(values, 0, 1, axis=along))
    return jnp.concatenate([rest, edge], axis=along)

def shift_behind(values, along):
    count = values.shape[along]
    rest = lax.slice_in_dim(values, 0, count - 1, axis=along)
    edge = jnp.zeros_like(lax.slice_in_dim(values, 0, 1, axis=along))
    return jnp.concatenate([edge, rest], axis=along)

def element_stiffness(densities, solid_mask, start_layer, total_layers):
    full_shape = densities.shape
    depth_index = lax.broadcasted_iota(jnp.int32, full_shape, 0) + start_layer
    across_x = lax.broadcasted_iota(jnp.int32, full_shape, 1)
    across_y = lax.broadcasted_iota(jnp.int32, full_shape, 2)
    inside = (depth_index < total_layers - 1) & (across_x < full_shape[1] - 1) & (across_y < full_shape[2] - 1)
    values = solid_mask.astype(jnp.float32) * densities ** 3 + void_stiffness
    return jnp.where(inside, values, 0.0)

def element_forces(extended, stiffness, matrix):
    layers = stiffness.shape[0]
    corner_views = []
    for c in range(8):
        view = lax.slice_in_dim(extended, c // 4, c // 4 + layers, axis=1)
        if c % 2:
            view = shift_ahead(view, 2)
        if c // 2 % 2:
            view = shift_ahead(view, 3)
        corner_views.append(view)
    stacked = jnp.stack(corner_views)
    forces = jnp.einsum('cadb,dbzxy->cazxy', matrix, stacked, precision=lax.Precision.HIGHEST) * stiffness
    result = jnp.zeros(extended.shape, jnp.float32)
    for c in range(8):
        piece = forces[c]
        if c % 2:
            piece = shift_behind(piece, 2)
        if c // 2 % 2:
            piece = shift_behind(piece, 3)
        result = result.at[:, c // 4:c // 4 + layers].add(piece)
    return result

def reference(recycle_basis, densities, solid_mask, fixed_mask):
    matrix = jnp.asarray(element_matrix(), dtype=jnp.float32)
    free_mask = 1.0 - fixed_mask.astype(jnp.float32)
    stiffness = element_stiffness(densities, solid_mask, 0, NZ)

    def image_of(column):
        moved = column * free_mask
        top_zero = jnp.zeros((column.shape[0], 1, column.shape[2], column.shape[3]), jnp.float32)
        extended = jnp.concatenate([moved, top_zero], axis=1)
        forces_out = element_forces(extended, stiffness, matrix)[:, :NZ]
        return free_mask * forces_out + fixed_mask.astype(jnp.float32) * column
    image_full = lax.map(image_of, recycle_basis)
    flattened = image_full.reshape(COLS, -1)
    gram_matrix = lax.dot_general(flattened.astype(jnp.float32), flattened.astype(jnp.float32), (((1,), (1,)), ((), ())), precision=lax.Precision.HIGHEST, preferred_element_type=jnp.float32) / ROWS
    cholesky_lower = jnp.linalg.cholesky(gram_matrix)
    inverse = lax.linalg.triangular_solve(cholesky_lower, jnp.eye(COLS, dtype=jnp.float32), left_side=True, lower=True)
    ortho = jnp.dot(inverse.astype(jnp.float32), flattened.astype(jnp.float32), precision=lax.Precision.HIGHEST, preferred_element_type=jnp.float32).reshape(recycle_basis.shape)
    renewed = jnp.dot(inverse.astype(jnp.float32), recycle_basis.reshape(COLS, -1).astype(jnp.float32), precision=lax.Precision.HIGHEST, preferred_element_type=jnp.float32).reshape(recycle_basis.shape)
    return (ortho, renewed, cholesky_lower.T)
```

```python
import functools

import jax
import jax.numpy as jnp
import numpy as np
from jax import lax
from jax.experimental import pallas as pl
from jax.experimental.pallas import tpu as pltpu
from jax.sharding import PartitionSpec as P

void_stiffness = 0.001
MESH = pl.DeviceIdType.MESH
f32 = jnp.float32


def element_matrix():
    poisson = 0.3
    lame_first = poisson / ((1.0 + poisson) * (1.0 - 2.0 * poisson))
    shear_mod = 1.0 / (2.0 * (1.0 + poisson))
    elastic = np.zeros((6, 6))
    elastic[:3, :3] = lame_first
    for k in range(3):
        elastic[k, k] = lame_first + 2.0 * shear_mod
    for k in range(3, 6):
        elastic[k, k] = shear_mod
    points = [(1.0 - 1.0 / np.sqrt(3.0)) / 2.0, (1.0 + 1.0 / np.sqrt(3.0)) / 2.0]
    matrix = np.zeros((24, 24))
    for a in points:
        for b in points:
            for d in points:
                strain = np.zeros((6, 24))
                for c in range(8):
                    ox, oy, oz = (c % 2, c // 2 % 2, c // 4)
                    weight_x = a if ox else 1.0 - a
                    weight_y = b if oy else 1.0 - b
                    weight_z = d if oz else 1.0 - d
                    slope_x = (1.0 if ox else -1.0) * weight_y * weight_z
                    slope_y = (1.0 if oy else -1.0) * weight_x * weight_z
                    slope_z = (1.0 if oz else -1.0) * weight_x * weight_y
                    strain[0, 3 * c] = slope_x
                    strain[1, 3 * c + 1] = slope_y
                    strain[2, 3 * c + 2] = slope_z
                    strain[3, 3 * c] = slope_y
                    strain[3, 3 * c + 1] = slope_x
                    strain[4, 3 * c + 1] = slope_z
                    strain[4, 3 * c + 2] = slope_y
                    strain[5, 3 * c] = slope_z
                    strain[5, 3 * c + 2] = slope_x
                matrix = matrix + strain.T @ elastic @ strain / 8.0
    return matrix.reshape(8, 3, 8, 3)


def mode_constants():
    signs = np.ones((8, 8))
    for m in range(8):
        for c in range(8):
            for bit in range(3):
                if m >> bit & 1 and not c >> bit & 1:
                    signs[m, c] *= -1.0
    modes = np.einsum("mc,cadb,nd->manb", signs, element_matrix(), signs) / 64.0
    alpha, beta = modes[1, 0, 1, 0], modes[1, 0, 2, 1]
    gamma, delta = modes[3, 1, 3, 1], modes[3, 1, 5, 2]
    shear, twist = modes[2, 0, 2, 0], modes[7, 2, 7, 2]
    eta_diag, eta = modes[6, 0, 6, 0], modes[6, 0, 5, 1]
    return [float(v) for v in (alpha - beta, beta, gamma, delta, shear, twist, eta_diag - eta, eta)]


def next_along_y(first, second, lane):
    a, b = (pltpu.roll(first, 127, axis=1), pltpu.roll(second, 127, axis=1))
    return (jnp.where(lane == 127, b, a), jnp.where(lane == 127, a, b))


def prior_along_y(first, second, lane):
    a, b = (pltpu.roll(first, 1, axis=1), pltpu.roll(second, 1, axis=1))
    return (jnp.where(lane == 0, b, a), jnp.where(lane == 0, a, b))


def column_image(layers, scaled, lane):
    fields = {}
    for l in range(4):
        for a in range(3):
            v = layers[l][a]
            halves = (v[:, :128], v[:, 128:])
            ahead = next_along_y(halves[0], halves[1], lane)
            for h in range(2):
                fields[l, a, h] = (halves[h] + ahead[h], ahead[h] - halves[h])

    def planes(l, a, h):
        out = []
        for f in fields[l, a, h]:
            g = pltpu.roll(f, 7, axis=0)
            out.append((f + g, g - f))
        return {0: out[0][0], 1: out[0][1], 2: out[1][0], 3: out[1][1]}

    partial = {}
    for h in range(2):
        below = [planes(0, a, h) for a in range(3)]
        acc = {}

        def add(key, value):
            acc[key] = acc[key] + value if key in acc else value

        for e in range(3):
            above = [planes(e + 1, a, h) for a in range(3)]

            def mode(a, m):
                lo, hi = (below[a][m & 3], above[a][m & 3])
                return hi - lo if m & 4 else hi + lo

            def stiff(k):
                return scaled[e, k, :, 128 * h : 128 * h + 128]

            force = {}
            x, y, z = (mode(0, 1), mode(1, 2), mode(2, 4))
            shared = (x + y + z) * stiff(1)
            force[0, 1] = x * stiff(0) + shared
            force[1, 2] = y * stiff(0) + shared
            force[2, 4] = z * stiff(0) + shared
            for a, b, p in ((1, 2, 1), (0, 2, 2), (0, 1, 4)):
                ma, mb = (p ^ (1 << a), p ^ (1 << b))
                q, r = (mode(a, ma), mode(b, mb))
                force[a, ma] = q * stiff(2) + r * stiff(3)
                force[b, mb] = r * stiff(2) + q * stiff(3)
            for a, b, c in ((0, 1, 2), (0, 2, 1), (1, 2, 0)):
                ma, mb = (1 << b, 1 << a)
                force[a, ma] = force[b, mb] = None
                both = (mode(a, ma) + mode(b, mb)) * stiff(4)
                force[a, ma] = force[b, mb] = both
                force[c, 7] = mode(c, 7) * stiff(5)
            x, y, z = (mode(0, 6), mode(1, 5), mode(2, 3))
            shared = (x + y + z) * stiff(7)
            force[0, 6] = x * stiff(6) + shared
            force[1, 5] = y * stiff(6) + shared
            force[2, 3] = z * stiff(6) + shared
            for a in range(3):
                for m in range(4):
                    high = force[a, m + 4]
                    low = force.get((a, m))
                    if e >= 1:
                        add((e - 1, a, m), -high if low is None else low - high)
                    if e <= 1:
                        add((e, a, m), high if low is None else low + high)
            below = above
        for l in range(2):
            for a in range(3):
                g = [acc[l, a, m] for m in range(4)]
                total = (g[0] - g[1]) + pltpu.roll(g[0] + g[1], 1, axis=0)
                slope = (g[2] - g[3]) + pltpu.roll(g[2] + g[3], 1, axis=0)
                partial[l, a, h] = (total - slope, total + slope)
    result = {}
    for l in range(2):
        for a in range(3):
            moved = prior_along_y(partial[l, a, 0][1], partial[l, a, 1][1], lane)
            result[l, a] = jnp.concatenate(
                [partial[l, a, 0][0] + moved[0], partial[l, a, 1][0] + moved[1]], axis=1
            )
    return result


def split_bf16(value, parts):
    out = []
    for _ in range(parts):
        piece = value.astype(jnp.bfloat16)
        out.append(piece)
        value = value - piece.astype(f32)
    return out


def body(
    slabs, cols, constants, rows_total,
    u_hbm, dens_hbm, solid_hbm, fixed_hbm,
    ortho_ref, renew_ref, r_ref,
    u_all, im_all, halo, dens, solid, fixed, scaled, gram_a, gram_b, rows_ref, coef_ref,
    local_sem, halo_send, halo_recv, ag_send, ag_recv, im_send, im_recv, ga_send, ga_recv, gb_send, gb_recv,
):
    s = lax.axis_index("slab")
    c = lax.axis_index("col")
    group = 8
    zi, yc = s // group, s % group
    zn = slabs // group

    def slab_at(value):
        return {"slab": value, "col": c}

    up, down = (lax.rem(s + 1, slabs), lax.rem(s + slabs - 1, slabs))
    partners = [slab_at(up), slab_at(down)]
    partners += [{"slab": s, "col": lax.rem(c + k, cols)} for k in range(1, cols)]
    partners += [slab_at(zi * group + lax.rem(yc + k, group)) for k in range(1, group)]
    partners += [slab_at(lax.rem(zi + k, zn) * group + yc) for k in range(1, zn)]

    local = [
        pltpu.make_async_copy(u_hbm, u_all.at[c], local_sem.at[0]),
        pltpu.make_async_copy(dens_hbm, dens.at[pl.ds(1, 2)], local_sem.at[1]),
        pltpu.make_async_copy(solid_hbm, solid.at[pl.ds(1, 2)], local_sem.at[2]),
        pltpu.make_async_copy(fixed_hbm, fixed.at[pl.ds(1, 2)], local_sem.at[3]),
    ]
    for copy in local:
        copy.start()

    barrier = pltpu.get_barrier_semaphore()
    for partner in partners:
        pl.semaphore_signal(barrier, inc=1, device_id=partner, device_id_type=MESH)
    pl.semaphore_wait(barrier, len(partners))

    def remote(src, dst, send, recv, where):
        return pltpu.make_async_remote_copy(
            src_ref=src, dst_ref=dst, send_sem=send, recv_sem=recv, device_id=where, device_id_type=MESH
        )

    halo_copies = []
    for k, (src, dst, where) in enumerate((
        (u_hbm.at[:, :, 1], halo.at[0], slab_at(up)),
        (u_hbm.at[:, :, 0], halo.at[1], slab_at(down)),
        (dens_hbm.at[1], dens.at[0], slab_at(up)),
        (solid_hbm.at[1], solid.at[0], slab_at(up)),
        (fixed_hbm.at[1], fixed.at[0], slab_at(up)),
        (fixed_hbm.at[0], fixed.at[3], slab_at(down)),
    )):
        halo_copies.append(remote(src, dst, halo_send.at[k], halo_recv.at[k], where))
    for copy in halo_copies:
        copy.start()

    ag_copies = [
        remote(u_hbm, u_all.at[c], ag_send.at[k], ag_recv.at[k], {"slab": s, "col": lax.rem(c + k, cols)})
        for k in range(1, cols)
    ]
    ag_copies[0].start()
    ag_copies[cols - 2].start()

    for copy in local:
        copy.wait()
    for copy in halo_copies:
        copy.wait()

    node = lax.broadcasted_iota(jnp.int32, (8, 256), 0)
    along = lax.broadcasted_iota(jnp.int32, (8, 256), 1)
    inside = (node < 7) & (along < 255)
    for e in range(3):
        depth = s * 2 - 1 + e
        value = solid[e].astype(f32) * (dens[e] * dens[e] * dens[e]) + void_stiffness
        keep = inside & (depth >= 0) & (depth < 2 * slabs - 1)
        value = jnp.where(keep, value, 0.0)
        for k, constant in enumerate(constants):
            scaled[e, k] = value * constant

    lane = lax.broadcasted_iota(jnp.int32, (8, 128), 1)

    def one_column(j, carry):
        free = [1.0 - fixed[l].astype(f32) for l in range(4)]
        raw = [[u_all[c, j, a, l] for a in range(3)] for l in range(2)]
        layers = [
            [halo[0, j, a] * free[0] for a in range(3)],
            [raw[0][a] * free[1] for a in range(3)],
            [raw[1][a] * free[2] for a in range(3)],
            [halo[1, j, a] * free[3] for a in range(3)],
        ]
        out = column_image(layers, scaled, lane)
        for l in range(2):
            for a in range(3):
                im_all[c, j, a, l] = free[l + 1] * out[l, a] + (1.0 - free[l + 1]) * raw[l][a]
        return carry

    lax.fori_loop(0, 4, one_column, 0)

    im_copies = [
        remote(im_all.at[c], im_all.at[c], im_send.at[k], im_recv.at[k], {"slab": s, "col": lax.rem(c + k, cols)})
        for k in range(1, cols)
    ]
    for copy in im_copies:
        copy.start()
    for copy in im_copies:
        copy.wait()
    for copy in ag_copies[1 : cols - 2]:
        copy.start()

    total = None
    for a in range(3):
        for l in range(2):
            block = im_all[:, :, a, l].reshape(128, 256)
            both = jnp.concatenate(split_bf16(block, 2), axis=0)
            part = lax.dot_general(both, both, (((1,), (1,)), ((), ())), preferred_element_type=f32)
            total = part if total is None else total + part
    pairs = (total[:128, :128] + total[128:, 128:]) + (total[:128, 128:] + total[128:, :128])
    row_id = lax.broadcasted_iota(jnp.int32, (128, 128), 0)
    col_id = lax.broadcasted_iota(jnp.int32, (128, 128), 1)
    pairs = jnp.where(row_id % 8 == col_id % 8, pairs, 0.0)
    partial = pairs.reshape(16, 8, 128).sum(axis=1)

    gram_a[yc] = partial
    ga_copies = [
        remote(gram_a.at[yc], gram_a.at[yc], ga_send.at[k], ga_recv.at[k], slab_at(zi * group + lax.rem(yc + k, group)))
        for k in range(1, group)
    ]
    for copy in ga_copies:
        copy.start()
    for copy in ga_copies:
        copy.wait()
    summed = gram_a[0]
    for k in range(1, group):
        summed = summed + gram_a[k]
    gram_b[zi] = summed
    gb_copies = [
        remote(gram_b.at[zi], gram_b.at[zi], gb_send.at[k], gb_recv.at[k], slab_at(lax.rem(zi + k, zn) * group + yc))
        for k in range(1, zn)
    ]
    for copy in gb_copies:
        copy.start()
    for copy in gb_copies:
        copy.wait()
    summed = gram_b[0]
    for k in range(1, zn):
        summed = summed + gram_b[k]

    picked = (row_id // 8 == col_id).astype(jnp.bfloat16)
    gram = None
    for piece in split_bf16(summed, 3)[::-1]:
        part = jnp.dot(piece, picked, preferred_element_type=f32)
        gram = part if gram is None else gram + part
    gram = gram * (1.0 / rows_total)

    row16 = lax.broadcasted_iota(jnp.int32, (16, 128), 0)
    lane16 = lax.broadcasted_iota(jnp.int32, (16, 128), 1)
    work = jnp.where(lane16 < 16, gram, (lane16 == row16 + 16).astype(f32))
    for k in range(16):
        pivot = work[k : k + 1, k : k + 1]
        scale = lax.rsqrt(pivot)
        scale = scale * (1.5 - 0.5 * pivot * scale * scale)
        row = work[k : k + 1, :] * scale
        rows_ref[k : k + 1, :] = row
        if k < 15:
            work = work - (work[:, k : k + 1] * scale) * row
    factor = rows_ref[...]
    r_ref[...] = jnp.where(lane16 >= row16, factor, 0.0)[:, :16]

    own = rows_ref[pl.ds(4 * c, 4), :]
    for i in range(4):
        for j in range(16):
            coef_ref[i, j] = jnp.broadcast_to(own[i : i + 1, 16 + j : 17 + j], (8, 256))

    for copy in ag_copies:
        copy.wait()

    def combine(step, carry):
        a, l = step // 2, step % 2
        for source, target in ((u_all, renew_ref), (im_all, ortho_ref)):
            acc = [None] * 4
            for j in range(16):
                value = source[j // 4, j % 4, a, l]
                for i in range(4):
                    term = coef_ref[i, j] * value
                    acc[i] = term if acc[i] is None else acc[i] + term
            for i in range(4):
                target[i, a, l] = acc[i]
        return carry

    lax.fori_loop(0, 6, combine, 0)


def solution(mesh):
    slabs, cols = (mesh.shape["slab"], mesh.shape["col"])
    constants = mode_constants()

    def on_device(recycle_basis, densities, solid_mask, fixed_mask):
        shape = recycle_basis.shape
        rows_total = 3 * slabs * shape[2] * shape[3] * shape[4]
        vmem = pl.BlockSpec(memory_space=pltpu.VMEM)
        hbm = pl.BlockSpec(memory_space=pl.ANY)
        dma = pltpu.SemaphoreType.DMA
        layer = shape[3:]
        return pl.pallas_call(
            functools.partial(body, slabs, cols, constants, float(rows_total)),
            out_shape=(
                jax.ShapeDtypeStruct(shape, f32),
                jax.ShapeDtypeStruct(shape, f32),
                jax.ShapeDtypeStruct((16, 16), f32),
            ),
            in_specs=[hbm] * 4,
            out_specs=(vmem, vmem, vmem),
            scratch_shapes=[
                pltpu.VMEM((cols,) + shape, f32),
                pltpu.VMEM((cols,) + shape, f32),
                pltpu.VMEM((2, 4, 3) + layer, f32),
                pltpu.VMEM((3,) + layer, f32),
                pltpu.VMEM((3,) + layer, jnp.int32),
                pltpu.VMEM((4,) + layer, jnp.int32),
                pltpu.VMEM((3, len(constants)) + layer, f32),
                pltpu.VMEM((8, 16, 128), f32),
                pltpu.VMEM((8, 16, 128), f32),
                pltpu.VMEM((16, 128), f32),
                pltpu.VMEM((4, 16, 8, 256), f32),
                dma((4,)), dma((6,)), dma((6,)),
                dma((4,)), dma((4,)), dma((4,)), dma((4,)),
                dma((8,)), dma((8,)), dma((8,)), dma((8,)),
            ],
            compiler_params=pltpu.CompilerParams(collective_id=0, has_side_effects=True),
        )(recycle_basis, densities, solid_mask, fixed_mask)

    placed = (
        P("col", None, "slab", None, None),
        P("slab", None, None),
        P("slab", None, None),
        P("slab", None, None),
    )
    return jax.shard_map(
        on_device,
        mesh=mesh,
        in_specs=placed,
        out_specs=(P("col", None, "slab", None, None), P("col", None, "slab", None, None), P()),
        check_vma=False,
    )
```

```python
import functools

import jax
import jax.numpy as jnp
import numpy as np
from jax import lax
from jax.experimental import pallas as pl
from jax.experimental.pallas import tpu as pltpu
from jax.sharding import PartitionSpec as P

void_stiffness = 0.001
MESH = pl.DeviceIdType.MESH
f32 = jnp.float32


def element_matrix():
    poisson = 0.3
    lame_first = poisson / ((1.0 + poisson) * (1.0 - 2.0 * poisson))
    shear_mod = 1.0 / (2.0 * (1.0 + poisson))
    elastic = np.zeros((6, 6))
    elastic[:3, :3] = lame_first
    for k in range(3):
        elastic[k, k] = lame_first + 2.0 * shear_mod
    for k in range(3, 6):
        elastic[k, k] = shear_mod
    points = [(1.0 - 1.0 / np.sqrt(3.0)) / 2.0, (1.0 + 1.0 / np.sqrt(3.0)) / 2.0]
    matrix = np.zeros((24, 24))
    for a in points:
        for b in points:
            for d in points:
                strain = np.zeros((6, 24))
                for c in range(8):
                    ox, oy, oz = (c % 2, c // 2 % 2, c // 4)
                    weight_x = a if ox else 1.0 - a
                    weight_y = b if oy else 1.0 - b
                    weight_z = d if oz else 1.0 - d
                    slope_x = (1.0 if ox else -1.0) * weight_y * weight_z
                    slope_y = (1.0 if oy else -1.0) * weight_x * weight_z
                    slope_z = (1.0 if oz else -1.0) * weight_x * weight_y
                    strain[0, 3 * c] = slope_x
                    strain[1, 3 * c + 1] = slope_y
                    strain[2, 3 * c + 2] = slope_z
                    strain[3, 3 * c] = slope_y
                    strain[3, 3 * c + 1] = slope_x
                    strain[4, 3 * c + 1] = slope_z
                    strain[4, 3 * c + 2] = slope_y
                    strain[5, 3 * c] = slope_z
                    strain[5, 3 * c + 2] = slope_x
                matrix = matrix + strain.T @ elastic @ strain / 8.0
    return matrix.reshape(8, 3, 8, 3)


def mode_constants():
    signs = np.ones((8, 8))
    for m in range(8):
        for c in range(8):
            for bit in range(3):
                if m >> bit & 1 and not c >> bit & 1:
                    signs[m, c] *= -1.0
    modes = np.einsum("mc,cadb,nd->manb", signs, element_matrix(), signs) / 64.0
    alpha, beta = modes[1, 0, 1, 0], modes[1, 0, 2, 1]
    gamma, delta = modes[3, 1, 3, 1], modes[3, 1, 5, 2]
    shear, twist = modes[2, 0, 2, 0], modes[7, 2, 7, 2]
    eta_diag, eta = modes[6, 0, 6, 0], modes[6, 0, 5, 1]
    return [float(v) for v in (alpha - beta, beta, gamma, delta, shear, twist, eta_diag - eta, eta)]


def next_along_y(first, second, lane):
    a, b = (pltpu.roll(first, 127, axis=1), pltpu.roll(second, 127, axis=1))
    return (jnp.where(lane == 127, b, a), jnp.where(lane == 127, a, b))


def prior_along_y(first, second, lane):
    a, b = (pltpu.roll(first, 1, axis=1), pltpu.roll(second, 1, axis=1))
    return (jnp.where(lane == 0, b, a), jnp.where(lane == 0, a, b))


def column_image(layers, scaled, lane):
    fields = {}
    for l in range(4):
        for a in range(3):
            v = layers[l][a]
            halves = (v[:, :128], v[:, 128:])
            ahead = next_along_y(halves[0], halves[1], lane)
            for h in range(2):
                fields[l, a, h] = (halves[h] + ahead[h], ahead[h] - halves[h])

    def planes(l, a, h):
        out = []
        for f in fields[l, a, h]:
            g = pltpu.roll(f, 7, axis=0)
            out.append((f + g, g - f))
        return {0: out[0][0], 1: out[0][1], 2: out[1][0], 3: out[1][1]}

    partial = {}
    for h in range(2):
        below = [planes(0, a, h) for a in range(3)]
        acc = {}

        def add(key, value):
            acc[key] = acc[key] + value if key in acc else value

        for e in range(3):
            above = [planes(e + 1, a, h) for a in range(3)]

            def mode(a, m):
                lo, hi = (below[a][m & 3], above[a][m & 3])
                return hi - lo if m & 4 else hi + lo

            def stiff(k):
                return scaled[e, k, :, 128 * h : 128 * h + 128]

            force = {}
            x, y, z = (mode(0, 1), mode(1, 2), mode(2, 4))
            shared = (x + y + z) * stiff(1)
            force[0, 1] = x * stiff(0) + shared
            force[1, 2] = y * stiff(0) + shared
            force[2, 4] = z * stiff(0) + shared
            for a, b, p in ((1, 2, 1), (0, 2, 2), (0, 1, 4)):
                ma, mb = (p ^ (1 << a), p ^ (1 << b))
                q, r = (mode(a, ma), mode(b, mb))
                force[a, ma] = q * stiff(2) + r * stiff(3)
                force[b, mb] = r * stiff(2) + q * stiff(3)
            for a, b, c in ((0, 1, 2), (0, 2, 1), (1, 2, 0)):
                ma, mb = (1 << b, 1 << a)
                force[a, ma] = force[b, mb] = None
                both = (mode(a, ma) + mode(b, mb)) * stiff(4)
                force[a, ma] = force[b, mb] = both
                force[c, 7] = mode(c, 7) * stiff(5)
            x, y, z = (mode(0, 6), mode(1, 5), mode(2, 3))
            shared = (x + y + z) * stiff(7)
            force[0, 6] = x * stiff(6) + shared
            force[1, 5] = y * stiff(6) + shared
            force[2, 3] = z * stiff(6) + shared
            for a in range(3):
                for m in range(4):
                    high = force[a, m + 4]
                    low = force.get((a, m))
                    if e >= 1:
                        add((e - 1, a, m), -high if low is None else low - high)
                    if e <= 1:
                        add((e, a, m), high if low is None else low + high)
            below = above
        for l in range(2):
            for a in range(3):
                g = [acc[l, a, m] for m in range(4)]
                total = (g[0] - g[1]) + pltpu.roll(g[0] + g[1], 1, axis=0)
                slope = (g[2] - g[3]) + pltpu.roll(g[2] + g[3], 1, axis=0)
                partial[l, a, h] = (total - slope, total + slope)
    result = {}
    for l in range(2):
        for a in range(3):
            moved = prior_along_y(partial[l, a, 0][1], partial[l, a, 1][1], lane)
            result[l, a] = jnp.concatenate(
                [partial[l, a, 0][0] + moved[0], partial[l, a, 1][0] + moved[1]], axis=1
            )
    return result


def split_bf16(value, parts):
    out = []
    for _ in range(parts):
        piece = value.astype(jnp.bfloat16)
        out.append(piece)
        value = value - piece.astype(f32)
    return out


def exact_dot(value, ones):
    rows = value.shape[0]
    parts = jnp.dot(jnp.concatenate(split_bf16(value, 3), axis=0), ones, preferred_element_type=f32)
    return (parts[2 * rows :] + parts[rows : 2 * rows]) + parts[:rows]


def exchange(
    slabs, cols, constants, rows_total,
    u_hbm, dens_hbm, solid_hbm, fixed_hbm,
    u_all, im_all, rows_ref,
    halo, dens, solid, fixed, scaled, gram_a, gram_b,
    local_sem, halo_send, halo_recv, u_send, u_recv, q_send, q_recv, im_send, im_recv, gram_send, gram_recv,
    ready_x, ready_z,
):
    s = lax.axis_index("slab")
    c = lax.axis_index("col")
    group = 8
    zi, yc = s // group, s % group
    zn = slabs // group
    wide = cols * group

    def at(slab, col):
        return {"slab": slab, "col": col}

    def along_x(k):
        return at(s, lax.rem(c + k + cols, cols))

    def along_z(k):
        return at(lax.rem(zi + k + zn, zn) * group + yc, c)

    up, down = (at(lax.rem(s + 1, slabs), c), at(lax.rem(s + slabs - 1, slabs), c))
    near = [up, down, along_z(1), along_z(-1)]
    near += [along_x(k) for k in range(1, cols)]
    near += [at(zi * group + lax.rem(yc + k, group), c) for k in range(1, group)]

    local = [
        pltpu.make_async_copy(u_hbm, u_all.at[c], local_sem.at[0]),
        pltpu.make_async_copy(dens_hbm, dens.at[pl.ds(1, 2)], local_sem.at[1]),
        pltpu.make_async_copy(solid_hbm, solid.at[pl.ds(1, 2)], local_sem.at[2]),
        pltpu.make_async_copy(fixed_hbm, fixed.at[pl.ds(1, 2)], local_sem.at[3]),
    ]
    barrier = pltpu.get_barrier_semaphore()
    for partner in near:
        pl.semaphore_signal(barrier, inc=1, device_id=partner, device_id_type=MESH)
    for copy in local:
        copy.start()
    pl.semaphore_wait(barrier, len(near))

    def remote(src, dst, send, recv, where):
        return pltpu.make_async_remote_copy(
            src_ref=src, dst_ref=dst, send_sem=send, recv_sem=recv, device_id=where, device_id_type=MESH
        )

    def received(ref, sem):
        remote(ref, ref, sem, sem, along_x(1)).wait_recv()

    def sent(ref, sem):
        remote(ref, ref, sem, sem, along_x(1)).wait_send()

    small_send, small_recv = (halo_send.at[4], halo_recv.at[4])
    remote(dens_hbm.at[1], dens.at[0], small_send, small_recv, up).start()
    remote(solid_hbm.at[1], solid.at[0], small_send, small_recv, up).start()
    remote(fixed_hbm.at[1], fixed.at[0], small_send, small_recv, up).start()
    remote(fixed_hbm.at[0], fixed.at[3], small_send, small_recv, down).start()
    for j in range(4):
        remote(u_hbm.at[j, :, 1], halo.at[0, j], halo_send.at[j], halo_recv.at[j], up).start()
        remote(u_hbm.at[j, :, 0], halo.at[1, j], halo_send.at[j], halo_recv.at[j], down).start()

    first_pair, last_pair = (pl.ds(0, 2), pl.ds(2, 2))
    u_next = remote(u_hbm, u_all.at[c], u_send.at[0], u_recv.at[0], along_x(1))
    u_wrap = remote(u_hbm, u_all.at[c], u_send.at[1], u_recv.at[1], along_x(-1))
    u_back = remote(u_hbm.at[last_pair], u_all.at[c, last_pair], u_send.at[2], u_recv.at[2], along_x(-1))
    pl.when(c < cols - 1)(u_next.start)
    pl.when(c == 0)(u_wrap.start)
    pl.when(c == 1)(u_back.start)

    for k in range(1, cols):
        pl.semaphore_signal(ready_x, inc=1, device_id=along_x(k), device_id_type=MESH)
    for k in (1, -1):
        pl.semaphore_signal(ready_z.at[0], inc=1, device_id=along_z(k), device_id_type=MESH)

    for copy in local:
        copy.wait()
    received(fixed, small_recv)

    node = lax.broadcasted_iota(jnp.int32, (8, 256), 0)
    along = lax.broadcasted_iota(jnp.int32, (8, 256), 1)
    inside = (node < 7) & (along < 255)
    for e in range(3):
        depth = s * 2 - 1 + e
        value = solid[e].astype(f32) * (dens[e] * dens[e] * dens[e]) + void_stiffness
        keep = inside & (depth >= 0) & (depth < 2 * slabs - 1)
        value = jnp.where(keep, value, 0.0)
        for k, constant in enumerate(constants):
            scaled[e, k] = value * constant

    lane = lax.broadcasted_iota(jnp.int32, (8, 128), 1)

    def one_column(j, carry):
        free = [1.0 - fixed[l].astype(f32) for l in range(4)]
        raw = [[u_all[c, j, a, l] for a in range(3)] for l in range(2)]
        received(halo.at[:, 0], halo_recv.at[j])
        layers = [
            [halo[0, j, a] * free[0] for a in range(3)],
            [raw[0][a] * free[1] for a in range(3)],
            [raw[1][a] * free[2] for a in range(3)],
            [halo[1, j, a] * free[3] for a in range(3)],
        ]
        out = column_image(layers, scaled, lane)
        for l in range(2):
            for a in range(3):
                value = free[l + 1] * out[l, a] + (1.0 - free[l + 1]) * raw[l][a]
                im_all[c, j, a, l, 0] = value[:, :128]
                im_all[c, j, a, l, 1] = value[:, 128:]
        for k in range(1, cols):
            t = lax.rem(c + k, cols)
            piece = im_all.at[c, j, :, t // 2, t % 2]
            remote(piece, piece, q_send, q_recv, at(s, t)).start()
        return carry

    lax.fori_loop(0, 4, one_column, 0)

    pl.semaphore_wait(ready_z.at[0], 2)
    for k in (2, -2):
        pl.semaphore_signal(ready_z.at[1], inc=1, device_id=along_z(k), device_id_type=MESH)
    pl.semaphore_wait(ready_x, cols - 1)

    quarters = im_all.at[pl.ds(0, cols - 1), :, :, 0, 0]
    received(quarters, q_recv)

    mine_l, mine_h = (c // 2, c % 2)
    sides = []
    for a in range(3):
        block = im_all[:, :, a, mine_l, mine_h].reshape(128, 128)
        sides.append(jnp.concatenate(split_bf16(block, 2), axis=0))
    total = None
    for both in (jnp.concatenate(sides[:2], axis=1), sides[2]):
        part = lax.dot_general(both, both, (((1,), (1,)), ((), ())), preferred_element_type=f32)
        total = part if total is None else total + part
    pairs = (total[:128, :128] + total[128:, 128:]) + (total[:128, 128:] + total[128:, :128])
    row_id = lax.broadcasted_iota(jnp.int32, (128, 128), 0)
    col_id = lax.broadcasted_iota(jnp.int32, (128, 128), 1)
    pairs = jnp.where(row_id % 8 == col_id % 8, pairs, 0.0).reshape(16, 8, 128).sum(axis=1)
    row16 = lax.broadcasted_iota(jnp.int32, (16, 128), 0)
    lane16 = lax.broadcasted_iota(jnp.int32, (16, 128), 1)
    spread = (row_id // 8 == col_id // 8).astype(jnp.bfloat16)
    pairs = exact_dot(pairs, spread)
    packed = jnp.where(row16 % 8 == lane16 % 8, pairs, 0.0).reshape(2, 8, 128).sum(axis=1)

    slot = c * group + yc
    gram_a[slot] = packed
    for k in range(1, wide):
        other = lax.rem(slot + k, wide)
        remote(
            gram_a.at[slot], gram_a.at[slot], gram_send.at[0], gram_recv.at[0], at(zi * group + other % group, other // group)
        ).start()

    for k in range(1, cols):
        t = lax.rem(c + 1 + k, cols)
        piece = im_all.at[c, :, :, t // 2, t % 2]
        pl.when(c < cols - 1)(remote(piece, piece, im_send.at[0], im_recv.at[0], along_x(1)).start)
        piece = im_all.at[c, :, :, (k - 1) // 2, (k - 1) % 2]
        pl.when(c == 0)(remote(piece, piece, im_send.at[1], im_recv.at[1], along_x(-1)).start)
    piece = im_all.at[c, :, :, 1, 0]
    im_back = remote(piece, piece, im_send.at[2], im_recv.at[2], along_x(-1))
    pl.when(c == 1)(im_back.start)

    ahead = (c == 1) | (c == 2)
    relay_block = jnp.where(ahead, c - 1, lax.rem(c + 1, cols))
    pl.when(c >= 1)(lambda: received(u_all.at[0], u_recv.at[0]))
    pl.when(c == 3)(lambda: received(u_all.at[0], u_recv.at[1]))
    pl.when(c == 0)(lambda: received(u_all.at[0, last_pair], u_recv.at[2]))
    ref = u_all.at[relay_block, first_pair]
    pl.when(ahead)(remote(ref, ref, u_send.at[3], u_recv.at[3], along_x(1)).start)
    ref = u_all.at[relay_block, last_pair]
    pl.when(jnp.logical_not(ahead))(remote(ref, ref, u_send.at[4], u_recv.at[4], along_x(-1)).start)

    received(gram_a.at[pl.ds(0, wide - 1)], gram_recv.at[0])
    summed = jnp.sum(gram_a[...], axis=0)
    gram_b[zi] = summed
    pl.semaphore_wait(ready_z.at[1], 2)
    for k in range(1, zn):
        remote(gram_b.at[zi], gram_b.at[zi], gram_send.at[1], gram_recv.at[1], along_z(k)).start()

    pl.when(c >= 1)(lambda: received(quarters, im_recv.at[0]))
    pl.when(c == 3)(lambda: received(quarters, im_recv.at[1]))
    pl.when(c == 0)(lambda: received(im_all.at[0, :, :, 0, 0], im_recv.at[2]))
    ref = im_all.at[relay_block, :, :, 0]
    pl.when(ahead)(remote(ref, ref, im_send.at[3], im_recv.at[3], along_x(1)).start)
    ref = im_all.at[relay_block, :, :, 1, jnp.where(c == 3, 1, 0)]
    pl.when(jnp.logical_not(ahead))(remote(ref, ref, im_send.at[4], im_recv.at[4], along_x(-1)).start)

    received(gram_b.at[pl.ds(0, zn - 1)], gram_recv.at[1])
    summed = jnp.sum(gram_b[...], axis=0)

    wide_rows = jnp.concatenate([jnp.broadcast_to(summed[r : r + 1], (8, 128)) for r in range(2)], axis=0)
    kept = jnp.where(row16 % 8 == lane16 % 8, wide_rows, 0.0)
    picked = (row_id // 8 == col_id).astype(jnp.bfloat16)
    gram = exact_dot(kept, picked) * (1.0 / rows_total)

    work = jnp.where(lane16 < 16, gram, (lane16 == row16 + 16).astype(f32))
    for k in range(16):
        pivot = work[k : k + 1, k : k + 1]
        scale = lax.rsqrt(pivot)
        scale = scale * (1.5 - 0.5 * pivot * scale * scale)
        row = work[k : k + 1, :] * scale
        rows_ref[k : k + 1, :] = row
        if k < 15:
            work = work - (work[:, k : k + 1] * scale) * row

    pl.when((c == 2) | (c == 3))(lambda: received(u_all.at[0, first_pair], u_recv.at[3]))
    pl.when((c == 2) | (c == 3))(lambda: received(u_all.at[0, first_pair], u_recv.at[4]))
    pl.when((c == 2) | (c == 3))(lambda: received(im_all.at[0, :, :, 0], im_recv.at[3]))
    pl.when((c == 2) | (c == 3))(lambda: received(im_all.at[0, :, :, 0, 0], im_recv.at[4]))
    sent(fixed, small_send)
    for j in range(4):
        sent(halo.at[:, 0], halo_send.at[j])
    sent(quarters, q_send)
    sent(gram_a.at[pl.ds(0, wide - 1)], gram_send.at[0])
    sent(gram_b.at[pl.ds(0, zn - 1)], gram_send.at[1])
    pl.when(c < cols - 1)(lambda: sent(u_all.at[0], u_send.at[0]))
    pl.when(c == 0)(lambda: sent(u_all.at[0], u_send.at[1]))
    pl.when(c == 1)(lambda: sent(u_all.at[0, first_pair], u_send.at[2]))
    pl.when(c < cols - 1)(lambda: sent(quarters, im_send.at[0]))
    pl.when(c == 0)(lambda: sent(quarters, im_send.at[1]))
    pl.when(c == 1)(lambda: sent(im_all.at[0, :, :, 0, 0], im_send.at[2]))
    pl.when(ahead)(lambda: sent(u_all.at[0, first_pair], u_send.at[3]))
    pl.when(ahead)(lambda: sent(im_all.at[0, :, :, 0], im_send.at[3]))
    pl.when(jnp.logical_not(ahead))(lambda: sent(u_all.at[0, first_pair], u_send.at[4]))
    pl.when(jnp.logical_not(ahead))(lambda: sent(im_all.at[0, :, :, 0, 0], im_send.at[4]))


def combine(u_all, im_all, rows_ref, ortho_hbm, renew_hbm, r_ref, ortho, renew, coef_ref, out_sem):
    c = lax.axis_index("col")
    row16 = lax.broadcasted_iota(jnp.int32, (16, 128), 0)
    lane16 = lax.broadcasted_iota(jnp.int32, (16, 128), 1)
    r_ref[...] = jnp.where(lane16 >= row16, rows_ref[...], 0.0)[:, :16]
    own = rows_ref[pl.ds(4 * c, 4), :]
    for i in range(4):
        for j in range(16):
            coef_ref[i, j] = jnp.broadcast_to(own[i : i + 1, 16 + j : 17 + j], (8, 128))

    def used(j, value):
        return value if j < 4 else jnp.where(j // 4 <= c, value, 0.0)

    def outputs(step):
        a, l = step // 2, step % 2
        return [
            pltpu.make_async_copy(ortho.at[:, a, l], ortho_hbm.at[:, a, l], out_sem.at[0]),
            pltpu.make_async_copy(renew.at[:, a, l], renew_hbm.at[:, a, l], out_sem.at[1]),
        ]

    def one(step, carry):
        a, l = step // 2, step % 2
        for h in range(2):
            for source, target in ((u_all, renew), (im_all, ortho)):
                acc = [None] * 4
                for j in range(16):
                    if source is u_all:
                        value = source[j // 4, j % 4, a, l, :, 128 * h : 128 * h + 128]
                    else:
                        value = source[j // 4, j % 4, a, l, h]
                    value = used(j, value)
                    for i in range(4):
                        term = coef_ref[i, j] * value
                        acc[i] = term if acc[i] is None else acc[i] + term
                for i in range(4):
                    target[i, a, l, :, 128 * h : 128 * h + 128] = acc[i]
        for copy in outputs(step):
            copy.start()
        return carry

    lax.fori_loop(0, 6, one, 0)
    pltpu.make_async_copy(ortho, ortho_hbm, out_sem.at[0]).wait()
    pltpu.make_async_copy(renew, renew_hbm, out_sem.at[1]).wait()


def solution(mesh):
    slabs, cols = (mesh.shape["slab"], mesh.shape["col"])
    constants = mode_constants()

    def on_device(recycle_basis, densities, solid_mask, fixed_mask):
        shape = recycle_basis.shape
        rows_total = 3 * slabs * shape[2] * shape[3] * shape[4]
        vmem = pl.BlockSpec(memory_space=pltpu.VMEM)
        hbm = pl.BlockSpec(memory_space=pl.ANY)
        dma = pltpu.SemaphoreType.DMA
        layer = shape[3:]
        u_all, im_all, rows = pl.pallas_call(
            functools.partial(exchange, slabs, cols, constants, float(rows_total)),
            out_shape=(
                pltpu.VMEM((cols,) + shape, f32),
                pltpu.VMEM((cols,) + shape[:3] + (2, 8, 128), f32),
                pltpu.VMEM((16, 128), f32),
            ),
            in_specs=[hbm] * 4,
            out_specs=(vmem, vmem, vmem),
            scratch_shapes=[
                pltpu.VMEM((2, 4, 3) + layer, f32),
                pltpu.VMEM((3,) + layer, f32),
                pltpu.VMEM((3,) + layer, jnp.int32),
                pltpu.VMEM((4,) + layer, jnp.int32),
                pltpu.VMEM((3, len(constants)) + layer, f32),
                pltpu.VMEM((cols * 8, 2, 128), f32),
                pltpu.VMEM((slabs // 8, 2, 128), f32),
                dma((4,)), dma((5,)), dma((5,)), dma((5,)), dma((5,)),
                dma, dma, dma((5,)), dma((5,)), dma((2,)), dma((2,)),
                pltpu.SemaphoreType.REGULAR, pltpu.SemaphoreType.REGULAR((2,)),
            ],
            compiler_params=pltpu.CompilerParams(collective_id=0, has_side_effects=True),
        )(recycle_basis, densities, solid_mask, fixed_mask)
        kept = [pltpu.with_memory_space_constraint(x, pltpu.VMEM) for x in (u_all, im_all, rows)]
        return pl.pallas_call(
            combine,
            out_shape=(
                jax.ShapeDtypeStruct(shape, f32),
                jax.ShapeDtypeStruct(shape, f32),
                jax.ShapeDtypeStruct((16, 16), f32),
            ),
            in_specs=[vmem] * 3,
            out_specs=(hbm, hbm, vmem),
            scratch_shapes=[
                pltpu.VMEM(shape, f32),
                pltpu.VMEM(shape, f32),
                pltpu.VMEM((4, 16, 8, 128), f32),
                dma((2,)),
            ],
        )(*kept)

    placed = (
        P("col", None, "slab", None, None),
        P("slab", None, None),
        P("slab", None, None),
        P("slab", None, None),
    )
    return jax.shard_map(
        on_device,
        mesh=mesh,
        in_specs=placed,
        out_specs=(P("col", None, "slab", None, None), P("col", None, "slab", None, None), P()),
        check_vma=False,
    )
```

```python
import functools

import jax
import jax.numpy as jnp
import numpy as np
from jax import lax
from jax.experimental import pallas as pl
from jax.experimental.pallas import tpu as pltpu
from jax.sharding import PartitionSpec as P

void_stiffness = 0.001
MESH = pl.DeviceIdType.MESH
f32 = jnp.float32


def element_matrix():
    poisson = 0.3
    lame_first = poisson / ((1.0 + poisson) * (1.0 - 2.0 * poisson))
    shear_mod = 1.0 / (2.0 * (1.0 + poisson))
    elastic = np.zeros((6, 6))
    elastic[:3, :3] = lame_first
    for k in range(3):
        elastic[k, k] = lame_first + 2.0 * shear_mod
    for k in range(3, 6):
        elastic[k, k] = shear_mod
    points = [(1.0 - 1.0 / np.sqrt(3.0)) / 2.0, (1.0 + 1.0 / np.sqrt(3.0)) / 2.0]
    matrix = np.zeros((24, 24))
    for a in points:
        for b in points:
            for d in points:
                strain = np.zeros((6, 24))
                for c in range(8):
                    ox, oy, oz = (c % 2, c // 2 % 2, c // 4)
                    weight_x = a if ox else 1.0 - a
                    weight_y = b if oy else 1.0 - b
                    weight_z = d if oz else 1.0 - d
                    slope_x = (1.0 if ox else -1.0) * weight_y * weight_z
                    slope_y = (1.0 if oy else -1.0) * weight_x * weight_z
                    slope_z = (1.0 if oz else -1.0) * weight_x * weight_y
                    strain[0, 3 * c] = slope_x
                    strain[1, 3 * c + 1] = slope_y
                    strain[2, 3 * c + 2] = slope_z
                    strain[3, 3 * c] = slope_y
                    strain[3, 3 * c + 1] = slope_x
                    strain[4, 3 * c + 1] = slope_z
                    strain[4, 3 * c + 2] = slope_y
                    strain[5, 3 * c] = slope_z
                    strain[5, 3 * c + 2] = slope_x
                matrix = matrix + strain.T @ elastic @ strain / 8.0
    return matrix.reshape(8, 3, 8, 3)


def mode_constants():
    signs = np.ones((8, 8))
    for m in range(8):
        for c in range(8):
            for bit in range(3):
                if m >> bit & 1 and not c >> bit & 1:
                    signs[m, c] *= -1.0
    modes = np.einsum("mc,cadb,nd->manb", signs, element_matrix(), signs) / 64.0
    alpha, beta = modes[1, 0, 1, 0], modes[1, 0, 2, 1]
    gamma, delta = modes[3, 1, 3, 1], modes[3, 1, 5, 2]
    shear, twist = modes[2, 0, 2, 0], modes[7, 2, 7, 2]
    eta_diag, eta = modes[6, 0, 6, 0], modes[6, 0, 5, 1]
    return [float(v) for v in (alpha - beta, beta, gamma, delta, shear, twist, eta_diag - eta, eta)]


def next_along_y(first, second, lane):
    a, b = (pltpu.roll(first, 127, axis=1), pltpu.roll(second, 127, axis=1))
    return (jnp.where(lane == 127, b, a), jnp.where(lane == 127, a, b))


def prior_along_y(first, second, lane):
    a, b = (pltpu.roll(first, 1, axis=1), pltpu.roll(second, 1, axis=1))
    return (jnp.where(lane == 0, b, a), jnp.where(lane == 0, a, b))


def column_image(layers, scaled, lane):
    fields = {}
    for l in range(4):
        for a in range(3):
            v = layers[l][a]
            halves = (v[:, :128], v[:, 128:])
            ahead = next_along_y(halves[0], halves[1], lane)
            for h in range(2):
                fields[l, a, h] = (halves[h] + ahead[h], ahead[h] - halves[h])

    def planes(l, a, h):
        out = []
        for f in fields[l, a, h]:
            g = pltpu.roll(f, 7, axis=0)
            out.append((f + g, g - f))
        return {0: out[0][0], 1: out[0][1], 2: out[1][0], 3: out[1][1]}

    partial = {}
    for h in range(2):
        below = [planes(0, a, h) for a in range(3)]
        acc = {}

        def add(key, value):
            acc[key] = acc[key] + value if key in acc else value

        for e in range(3):
            above = [planes(e + 1, a, h) for a in range(3)]

            def mode(a, m):
                lo, hi = (below[a][m & 3], above[a][m & 3])
                return hi - lo if m & 4 else hi + lo

            def stiff(k):
                return scaled[e, k, :, 128 * h : 128 * h + 128]

            force = {}
            x, y, z = (mode(0, 1), mode(1, 2), mode(2, 4))
            shared = (x + y + z) * stiff(1)
            force[0, 1] = x * stiff(0) + shared
            force[1, 2] = y * stiff(0) + shared
            force[2, 4] = z * stiff(0) + shared
            for a, b, p in ((1, 2, 1), (0, 2, 2), (0, 1, 4)):
                ma, mb = (p ^ (1 << a), p ^ (1 << b))
                q, r = (mode(a, ma), mode(b, mb))
                force[a, ma] = q * stiff(2) + r * stiff(3)
                force[b, mb] = r * stiff(2) + q * stiff(3)
            for a, b, c in ((0, 1, 2), (0, 2, 1), (1, 2, 0)):
                ma, mb = (1 << b, 1 << a)
                force[a, ma] = force[b, mb] = None
                both = (mode(a, ma) + mode(b, mb)) * stiff(4)
                force[a, ma] = force[b, mb] = both
                force[c, 7] = mode(c, 7) * stiff(5)
            x, y, z = (mode(0, 6), mode(1, 5), mode(2, 3))
            shared = (x + y + z) * stiff(7)
            force[0, 6] = x * stiff(6) + shared
            force[1, 5] = y * stiff(6) + shared
            force[2, 3] = z * stiff(6) + shared
            for a in range(3):
                for m in range(4):
                    high = force[a, m + 4]
                    low = force.get((a, m))
                    if e >= 1:
                        add((e - 1, a, m), -high if low is None else low - high)
                    if e <= 1:
                        add((e, a, m), high if low is None else low + high)
            below = above
        for l in range(2):
            for a in range(3):
                g = [acc[l, a, m] for m in range(4)]
                total = (g[0] - g[1]) + pltpu.roll(g[0] + g[1], 1, axis=0)
                slope = (g[2] - g[3]) + pltpu.roll(g[2] + g[3], 1, axis=0)
                partial[l, a, h] = (total - slope, total + slope)
    result = {}
    for l in range(2):
        for a in range(3):
            moved = prior_along_y(partial[l, a, 0][1], partial[l, a, 1][1], lane)
            result[l, a] = jnp.concatenate(
                [partial[l, a, 0][0] + moved[0], partial[l, a, 1][0] + moved[1]], axis=1
            )
    return result


def split_bf16(value, parts):
    out = []
    for _ in range(parts):
        piece = value.astype(jnp.bfloat16)
        out.append(piece)
        value = value - piece.astype(f32)
    return out


def exact_dot(value, ones):
    rows = value.shape[0]
    parts = jnp.dot(jnp.concatenate(split_bf16(value, 3), axis=0), ones, preferred_element_type=f32)
    return (parts[2 * rows :] + parts[rows : 2 * rows]) + parts[:rows]


def exchange(
    slabs, cols, constants, rows_total,
    u_hbm, dens_hbm, solid_hbm, fixed_hbm,
    u_all, im_all, rows_ref,
    halo, dens, solid, fixed, scaled, gram_a, gram_b,
    local_sem, halo_send, halo_recv, u_send, u_recv, q_send, q_recv, im_send, im_recv, gram_send, gram_recv,
    ready_x, ready_z,
):
    s = lax.axis_index("slab")
    c = lax.axis_index("col")
    group = 8
    zi, yc = s // group, s % group
    zn = slabs // group
    wide = cols * group

    def at(slab, col):
        return {"slab": slab, "col": col}

    def along_x(k):
        return at(s, lax.rem(c + k + cols, cols))

    def along_z(k):
        return at(lax.rem(zi + k + zn, zn) * group + yc, c)

    up, down = (at(lax.rem(s + 1, slabs), c), at(lax.rem(s + slabs - 1, slabs), c))
    near = [up, down, along_z(1), along_z(-1)]
    near += [along_x(k) for k in range(1, cols)]
    near += [at(zi * group + lax.rem(yc + k, group), c) for k in range(1, group)]

    local = [
        pltpu.make_async_copy(u_hbm, u_all.at[c], local_sem.at[0]),
        pltpu.make_async_copy(dens_hbm, dens.at[pl.ds(1, 2)], local_sem.at[1]),
        pltpu.make_async_copy(solid_hbm, solid.at[pl.ds(1, 2)], local_sem.at[2]),
        pltpu.make_async_copy(fixed_hbm, fixed.at[pl.ds(1, 2)], local_sem.at[3]),
    ]
    barrier = pltpu.get_barrier_semaphore()
    for partner in near:
        pl.semaphore_signal(barrier, inc=1, device_id=partner, device_id_type=MESH)
    for copy in local:
        copy.start()
    pl.semaphore_wait(barrier, len(near))

    def remote(src, dst, send, recv, where):
        return pltpu.make_async_remote_copy(
            src_ref=src, dst_ref=dst, send_sem=send, recv_sem=recv, device_id=where, device_id_type=MESH
        )

    def received(ref, sem):
        remote(ref, ref, sem, sem, along_x(1)).wait_recv()

    def sent(ref, sem):
        remote(ref, ref, sem, sem, along_x(1)).wait_send()

    small_send, small_recv = (halo_send.at[4], halo_recv.at[4])
    remote(dens_hbm.at[1], dens.at[0], small_send, small_recv, up).start()
    remote(solid_hbm.at[1], solid.at[0], small_send, small_recv, up).start()
    remote(fixed_hbm.at[1], fixed.at[0], small_send, small_recv, up).start()
    remote(fixed_hbm.at[0], fixed.at[3], small_send, small_recv, down).start()
    for j in range(4):
        remote(u_hbm.at[j, :, 1], halo.at[0, j], halo_send.at[j], halo_recv.at[j], up).start()
        remote(u_hbm.at[j, :, 0], halo.at[1, j], halo_send.at[j], halo_recv.at[j], down).start()

    first_pair, last_pair = (pl.ds(0, 2), pl.ds(2, 2))
    def share(part):
        ref = u_all.at[c, part]
        pl.when(c < cols - 1)(remote(u_hbm.at[part], ref, u_send.at[0], u_recv.at[0], along_x(1)).start)
        pl.when(c == 0)(remote(u_hbm.at[part], ref, u_send.at[1], u_recv.at[1], along_x(-1)).start)

    share(pl.ds(0, 3))

    for k in range(1, cols):
        pl.semaphore_signal(ready_x, inc=1, device_id=along_x(k), device_id_type=MESH)
    for k in (1, -1):
        pl.semaphore_signal(ready_z.at[0], inc=1, device_id=along_z(k), device_id_type=MESH)

    for copy in local:
        copy.wait()
    received(fixed, small_recv)

    node = lax.broadcasted_iota(jnp.int32, (8, 256), 0)
    along = lax.broadcasted_iota(jnp.int32, (8, 256), 1)
    inside = (node < 7) & (along < 255)
    for e in range(3):
        depth = s * 2 - 1 + e
        value = solid[e].astype(f32) * (dens[e] * dens[e] * dens[e]) + void_stiffness
        keep = inside & (depth >= 0) & (depth < 2 * slabs - 1)
        value = jnp.where(keep, value, 0.0)
        for k, constant in enumerate(constants):
            scaled[e, k] = value * constant

    lane = lax.broadcasted_iota(jnp.int32, (8, 128), 1)

    def one_column(j, carry):
        free = [1.0 - fixed[l].astype(f32) for l in range(4)]
        raw = [[u_all[c, j, a, l] for a in range(3)] for l in range(2)]
        received(halo.at[:, 0], halo_recv.at[j])
        layers = [
            [halo[0, j, a] * free[0] for a in range(3)],
            [raw[0][a] * free[1] for a in range(3)],
            [raw[1][a] * free[2] for a in range(3)],
            [halo[1, j, a] * free[3] for a in range(3)],
        ]
        out = column_image(layers, scaled, lane)
        for l in range(2):
            for a in range(3):
                value = free[l + 1] * out[l, a] + (1.0 - free[l + 1]) * raw[l][a]
                im_all[c, j, a, l, 0] = value[:, :128]
                im_all[c, j, a, l, 1] = value[:, 128:]
        for k in (2, 1, 3):
            t = lax.rem(c + k, cols)
            piece = im_all.at[c, j, :, t // 2, t % 2]
            remote(piece, piece, q_send, q_recv, at(s, t)).start()
        return carry

    lax.fori_loop(0, 4, one_column, 0)

    share(pl.ds(3, 1))
    u_back = remote(u_hbm.at[last_pair], u_all.at[c, last_pair], u_send.at[2], u_recv.at[2], along_x(-1))
    pl.when(c == 1)(u_back.start)

    pl.semaphore_wait(ready_z.at[0], 2)
    for k in (2, -2):
        pl.semaphore_signal(ready_z.at[1], inc=1, device_id=along_z(k), device_id_type=MESH)
    pl.semaphore_wait(ready_x, cols - 1)

    quarters = im_all.at[pl.ds(0, cols - 1), :, :, 0, 0]
    received(quarters, q_recv)

    mine_l, mine_h = (c // 2, c % 2)
    sides = []
    for a in range(3):
        block = im_all[:, :, a, mine_l, mine_h].reshape(128, 128)
        sides.append(jnp.concatenate(split_bf16(block, 2), axis=0))
    total = None
    for both in (jnp.concatenate(sides[:2], axis=1), sides[2]):
        part = lax.dot_general(both, both, (((1,), (1,)), ((), ())), preferred_element_type=f32)
        total = part if total is None else total + part
    pairs = (total[:128, :128] + total[128:, 128:]) + (total[:128, 128:] + total[128:, :128])
    row_id = lax.broadcasted_iota(jnp.int32, (128, 128), 0)
    col_id = lax.broadcasted_iota(jnp.int32, (128, 128), 1)
    pairs = jnp.where(row_id % 8 == col_id % 8, pairs, 0.0).reshape(16, 8, 128).sum(axis=1)
    row16 = lax.broadcasted_iota(jnp.int32, (16, 128), 0)
    lane16 = lax.broadcasted_iota(jnp.int32, (16, 128), 1)
    spread = (row_id // 8 == col_id // 8).astype(jnp.bfloat16)
    pairs = exact_dot(pairs, spread)
    packed = jnp.where(row16 % 8 == lane16 % 8, pairs, 0.0).reshape(2, 8, 128).sum(axis=1)

    slot = c * group + yc
    gram_a[slot] = packed
    hops = [(min(k, cols - k) + min(m // 2, group // 2 - m // 2), k, m) for k in range(cols) for m in range(group)]
    for _, k, m in sorted(hops, reverse=True)[:-1]:
        where = at(zi * group + lax.rem(yc + m, group), lax.rem(c + k, cols))
        remote(gram_a.at[slot], gram_a.at[slot], gram_send.at[0], gram_recv.at[0], where).start()

    for k in range(1, cols):
        t = lax.rem(c + 1 + k, cols)
        piece = im_all.at[c, :, :, t // 2, t % 2]
        pl.when(c < cols - 1)(remote(piece, piece, im_send.at[0], im_recv.at[0], along_x(1)).start)
        piece = im_all.at[c, :, :, (k - 1) // 2, (k - 1) % 2]
        pl.when(c == 0)(remote(piece, piece, im_send.at[1], im_recv.at[1], along_x(-1)).start)
    piece = im_all.at[c, :, :, 1, 0]
    im_back = remote(piece, piece, im_send.at[2], im_recv.at[2], along_x(-1))
    pl.when(c == 1)(im_back.start)

    ahead = (c == 1) | (c == 2)
    relay_block = jnp.where(ahead, c - 1, lax.rem(c + 1, cols))
    pl.when(c >= 1)(lambda: received(u_all.at[0], u_recv.at[0]))
    pl.when(c == 3)(lambda: received(u_all.at[0], u_recv.at[1]))
    pl.when(c == 0)(lambda: received(u_all.at[0, last_pair], u_recv.at[2]))
    ref = u_all.at[relay_block, first_pair]
    pl.when(ahead)(remote(ref, ref, u_send.at[3], u_recv.at[3], along_x(1)).start)
    ref = u_all.at[relay_block, last_pair]
    pl.when(jnp.logical_not(ahead))(remote(ref, ref, u_send.at[4], u_recv.at[4], along_x(-1)).start)

    received(gram_a.at[pl.ds(0, wide - 1)], gram_recv.at[0])
    summed = jnp.sum(gram_a[...], axis=0)
    gram_b[zi] = summed
    pl.semaphore_wait(ready_z.at[1], 2)
    for k in sorted(range(1, zn), key=lambda k: -min(k, zn - k)):
        remote(gram_b.at[zi], gram_b.at[zi], gram_send.at[1], gram_recv.at[1], along_z(k)).start()

    pl.when(c >= 1)(lambda: received(quarters, im_recv.at[0]))
    pl.when(c == 3)(lambda: received(quarters, im_recv.at[1]))
    pl.when(c == 0)(lambda: received(im_all.at[0, :, :, 0, 0], im_recv.at[2]))
    ref = im_all.at[relay_block, :, :, 0]
    pl.when(ahead)(remote(ref, ref, im_send.at[3], im_recv.at[3], along_x(1)).start)
    ref = im_all.at[relay_block, :, :, 1, jnp.where(c == 3, 1, 0)]
    pl.when(jnp.logical_not(ahead))(remote(ref, ref, im_send.at[4], im_recv.at[4], along_x(-1)).start)

    received(gram_b.at[pl.ds(0, zn - 1)], gram_recv.at[1])
    summed = jnp.sum(gram_b[...], axis=0)

    wide_rows = jnp.concatenate([jnp.broadcast_to(summed[r : r + 1], (8, 128)) for r in range(2)], axis=0)
    kept = jnp.where(row16 % 8 == lane16 % 8, wide_rows, 0.0)
    picked = (row_id // 8 == col_id).astype(jnp.bfloat16)
    gram = exact_dot(kept, picked) * (1.0 / rows_total)

    work = jnp.where(lane16 < 16, gram, (lane16 == row16 + 16).astype(f32))
    for first in range(0, 16, 4):
        ids = range(4)
        side = [jnp.broadcast_to(work[:, first + b : first + b + 1], (16, 128)) for b in ids]
        rows = [work[first + a : first + a + 1] for a in ids]
        low = {}
        scale = []
        for b in ids:
            for a in range(b, 4):
                value = side[b][first + a : first + a + 1]
                for d in range(b):
                    value = value - low[a, d] * low[b, d]
                if a == b:
                    scale.append(lax.rsqrt(value))
                else:
                    low[a, b] = value * scale[b]
        for b in ids:
            for d in range(b):
                rows[b] = rows[b] - low[b, d] * rows[d]
                side[b] = side[b] - side[d] * low[b, d]
            rows[b] = rows[b] * scale[b]
            side[b] = side[b] * scale[b]
            rows_ref[first + b : first + b + 1, :] = rows[b]
        if first < 12:
            work = work - ((side[0] * rows[0] + side[1] * rows[1]) + (side[2] * rows[2] + side[3] * rows[3]))

    pl.when((c == 2) | (c == 3))(lambda: received(u_all.at[0, first_pair], u_recv.at[3]))
    pl.when((c == 2) | (c == 3))(lambda: received(u_all.at[0, first_pair], u_recv.at[4]))
    pl.when((c == 2) | (c == 3))(lambda: received(im_all.at[0, :, :, 0], im_recv.at[3]))
    pl.when((c == 2) | (c == 3))(lambda: received(im_all.at[0, :, :, 0, 0], im_recv.at[4]))
    sent(fixed, small_send)
    for j in range(4):
        sent(halo.at[:, 0], halo_send.at[j])
    sent(quarters, q_send)
    sent(gram_a.at[pl.ds(0, wide - 1)], gram_send.at[0])
    sent(gram_b.at[pl.ds(0, zn - 1)], gram_send.at[1])
    pl.when(c < cols - 1)(lambda: sent(u_all.at[0], u_send.at[0]))
    pl.when(c == 0)(lambda: sent(u_all.at[0], u_send.at[1]))
    pl.when(c == 1)(lambda: sent(u_all.at[0, first_pair], u_send.at[2]))
    pl.when(c < cols - 1)(lambda: sent(quarters, im_send.at[0]))
    pl.when(c == 0)(lambda: sent(quarters, im_send.at[1]))
    pl.when(c == 1)(lambda: sent(im_all.at[0, :, :, 0, 0], im_send.at[2]))
    pl.when(ahead)(lambda: sent(u_all.at[0, first_pair], u_send.at[3]))
    pl.when(ahead)(lambda: sent(im_all.at[0, :, :, 0], im_send.at[3]))
    pl.when(jnp.logical_not(ahead))(lambda: sent(u_all.at[0, first_pair], u_send.at[4]))
    pl.when(jnp.logical_not(ahead))(lambda: sent(im_all.at[0, :, :, 0, 0], im_send.at[4]))


def combine(u_all, im_all, rows_ref, ortho_hbm, renew_hbm, r_ref, ortho, renew, coef_ref, out_sem):
    c = lax.axis_index("col")
    row16 = lax.broadcasted_iota(jnp.int32, (16, 128), 0)
    lane16 = lax.broadcasted_iota(jnp.int32, (16, 128), 1)
    r_ref[...] = jnp.where(lane16 >= row16, rows_ref[...], 0.0)[:, :16]
    own = rows_ref[pl.ds(4 * c, 4), :]
    for i in range(4):
        for j in range(16):
            coef_ref[i, j] = jnp.broadcast_to(own[i : i + 1, 16 + j : 17 + j], (8, 128))

    def used(j, value):
        return value if j < 4 else jnp.where(j // 4 <= c, value, 0.0)

    def outputs(step):
        a, l = step // 2, step % 2
        return [
            pltpu.make_async_copy(ortho.at[:, a, l], ortho_hbm.at[:, a, l], out_sem.at[0]),
            pltpu.make_async_copy(renew.at[:, a, l], renew_hbm.at[:, a, l], out_sem.at[1]),
        ]

    def one(step, carry):
        a, l = step // 2, step % 2
        for h in range(2):
            for source, target in ((u_all, renew), (im_all, ortho)):
                acc = [None] * 4
                for j in range(16):
                    if source is u_all:
                        value = source[j // 4, j % 4, a, l, :, 128 * h : 128 * h + 128]
                    else:
                        value = source[j // 4, j % 4, a, l, h]
                    value = used(j, value)
                    for i in range(4):
                        term = coef_ref[i, j] * value
                        acc[i] = term if acc[i] is None else acc[i] + term
                for i in range(4):
                    target[i, a, l, :, 128 * h : 128 * h + 128] = acc[i]
        for copy in outputs(step):
            copy.start()
        return carry

    lax.fori_loop(0, 6, one, 0)
    pltpu.make_async_copy(ortho, ortho_hbm, out_sem.at[0]).wait()
    pltpu.make_async_copy(renew, renew_hbm, out_sem.at[1]).wait()


def solution(mesh):
    slabs, cols = (mesh.shape["slab"], mesh.shape["col"])
    constants = mode_constants()

    def on_device(recycle_basis, densities, solid_mask, fixed_mask):
        shape = recycle_basis.shape
        rows_total = 3 * slabs * shape[2] * shape[3] * shape[4]
        vmem = pl.BlockSpec(memory_space=pltpu.VMEM)
        hbm = pl.BlockSpec(memory_space=pl.ANY)
        dma = pltpu.SemaphoreType.DMA
        layer = shape[3:]
        u_all, im_all, rows = pl.pallas_call(
            functools.partial(exchange, slabs, cols, constants, float(rows_total)),
            out_shape=(
                pltpu.VMEM((cols,) + shape, f32),
                pltpu.VMEM((cols,) + shape[:3] + (2, 8, 128), f32),
                pltpu.VMEM((16, 128), f32),
            ),
            in_specs=[hbm] * 4,
            out_specs=(vmem, vmem, vmem),
            scratch_shapes=[
                pltpu.VMEM((2, 4, 3) + layer, f32),
                pltpu.VMEM((3,) + layer, f32),
                pltpu.VMEM((3,) + layer, jnp.int32),
                pltpu.VMEM((4,) + layer, jnp.int32),
                pltpu.VMEM((3, len(constants)) + layer, f32),
                pltpu.VMEM((cols * 8, 2, 128), f32),
                pltpu.VMEM((slabs // 8, 2, 128), f32),
                dma((4,)), dma((5,)), dma((5,)), dma((5,)), dma((5,)),
                dma, dma, dma((5,)), dma((5,)), dma((2,)), dma((2,)),
                pltpu.SemaphoreType.REGULAR, pltpu.SemaphoreType.REGULAR((2,)),
            ],
            compiler_params=pltpu.CompilerParams(collective_id=0, has_side_effects=True),
        )(recycle_basis, densities, solid_mask, fixed_mask)
        kept = [pltpu.with_memory_space_constraint(x, pltpu.VMEM) for x in (u_all, im_all, rows)]
        return pl.pallas_call(
            combine,
            out_shape=(
                jax.ShapeDtypeStruct(shape, f32),
                jax.ShapeDtypeStruct(shape, f32),
                jax.ShapeDtypeStruct((16, 16), f32),
            ),
            in_specs=[vmem] * 3,
            out_specs=(hbm, hbm, vmem),
            scratch_shapes=[
                pltpu.VMEM(shape, f32),
                pltpu.VMEM(shape, f32),
                pltpu.VMEM((4, 16, 8, 128), f32),
                dma((2,)),
            ],
        )(*kept)

    placed = (
        P("col", None, "slab", None, None),
        P("slab", None, None),
        P("slab", None, None),
        P("slab", None, None),
    )
    return jax.shard_map(
        on_device,
        mesh=mesh,
        in_specs=placed,
        out_specs=(P("col", None, "slab", None, None), P("col", None, "slab", None, None), P()),
        check_vma=False,
    )
```

```python
import functools

import jax
import jax.numpy as jnp
import numpy as np
from jax import lax
from jax.experimental import pallas as pl
from jax.experimental.pallas import tpu as pltpu
from jax.sharding import PartitionSpec as P

void_stiffness = 0.001
MESH = pl.DeviceIdType.MESH
f32 = jnp.float32


def element_matrix():
    poisson = 0.3
    lame_first = poisson / ((1.0 + poisson) * (1.0 - 2.0 * poisson))
    shear_mod = 1.0 / (2.0 * (1.0 + poisson))
    elastic = np.zeros((6, 6))
    elastic[:3, :3] = lame_first
    for k in range(3):
        elastic[k, k] = lame_first + 2.0 * shear_mod
    for k in range(3, 6):
        elastic[k, k] = shear_mod
    points = [(1.0 - 1.0 / np.sqrt(3.0)) / 2.0, (1.0 + 1.0 / np.sqrt(3.0)) / 2.0]
    matrix = np.zeros((24, 24))
    for a in points:
        for b in points:
            for d in points:
                strain = np.zeros((6, 24))
                for c in range(8):
                    ox, oy, oz = (c % 2, c // 2 % 2, c // 4)
                    weight_x = a if ox else 1.0 - a
                    weight_y = b if oy else 1.0 - b
                    weight_z = d if oz else 1.0 - d
                    slope_x = (1.0 if ox else -1.0) * weight_y * weight_z
                    slope_y = (1.0 if oy else -1.0) * weight_x * weight_z
                    slope_z = (1.0 if oz else -1.0) * weight_x * weight_y
                    strain[0, 3 * c] = slope_x
                    strain[1, 3 * c + 1] = slope_y
                    strain[2, 3 * c + 2] = slope_z
                    strain[3, 3 * c] = slope_y
                    strain[3, 3 * c + 1] = slope_x
                    strain[4, 3 * c + 1] = slope_z
                    strain[4, 3 * c + 2] = slope_y
                    strain[5, 3 * c] = slope_z
                    strain[5, 3 * c + 2] = slope_x
                matrix = matrix + strain.T @ elastic @ strain / 8.0
    return matrix.reshape(8, 3, 8, 3)


def mode_constants():
    signs = np.ones((8, 8))
    for m in range(8):
        for c in range(8):
            for bit in range(3):
                if m >> bit & 1 and not c >> bit & 1:
                    signs[m, c] *= -1.0
    modes = np.einsum("mc,cadb,nd->manb", signs, element_matrix(), signs) / 64.0
    alpha, beta = modes[1, 0, 1, 0], modes[1, 0, 2, 1]
    gamma, delta = modes[3, 1, 3, 1], modes[3, 1, 5, 2]
    shear, twist = modes[2, 0, 2, 0], modes[7, 2, 7, 2]
    eta_diag, eta = modes[6, 0, 6, 0], modes[6, 0, 5, 1]
    return [float(v) for v in (alpha - beta, beta, gamma, delta, shear, twist, eta_diag - eta, eta)]


def next_along_y(first, second, lane):
    a, b = (pltpu.roll(first, 127, axis=1), pltpu.roll(second, 127, axis=1))
    return (jnp.where(lane == 127, b, a), jnp.where(lane == 127, a, b))


def prior_along_y(first, second, lane):
    a, b = (pltpu.roll(first, 1, axis=1), pltpu.roll(second, 1, axis=1))
    return (jnp.where(lane == 0, b, a), jnp.where(lane == 0, a, b))


def column_image(layers, scaled, lane):
    fields = {}
    for l in range(4):
        for a in range(3):
            v = layers[l][a]
            halves = (v[:, :128], v[:, 128:])
            ahead = next_along_y(halves[0], halves[1], lane)
            for h in range(2):
                fields[l, a, h] = (halves[h] + ahead[h], ahead[h] - halves[h])

    def planes(l, a, h):
        out = []
        for f in fields[l, a, h]:
            g = pltpu.roll(f, 7, axis=0)
            out.append((f + g, g - f))
        return {0: out[0][0], 1: out[0][1], 2: out[1][0], 3: out[1][1]}

    partial = {}
    for h in range(2):
        below = [planes(0, a, h) for a in range(3)]
        acc = {}

        def add(key, value):
            acc[key] = acc[key] + value if key in acc else value

        for e in range(3):
            above = [planes(e + 1, a, h) for a in range(3)]

            def mode(a, m):
                lo, hi = (below[a][m & 3], above[a][m & 3])
                return hi - lo if m & 4 else hi + lo

            def stiff(k):
                return scaled[e, k, :, 128 * h : 128 * h + 128]

            force = {}
            x, y, z = (mode(0, 1), mode(1, 2), mode(2, 4))
            shared = (x + y + z) * stiff(1)
            force[0, 1] = x * stiff(0) + shared
            force[1, 2] = y * stiff(0) + shared
            force[2, 4] = z * stiff(0) + shared
            for a, b, p in ((1, 2, 1), (0, 2, 2), (0, 1, 4)):
                ma, mb = (p ^ (1 << a), p ^ (1 << b))
                q, r = (mode(a, ma), mode(b, mb))
                force[a, ma] = q * stiff(2) + r * stiff(3)
                force[b, mb] = r * stiff(2) + q * stiff(3)
            for a, b, c in ((0, 1, 2), (0, 2, 1), (1, 2, 0)):
                ma, mb = (1 << b, 1 << a)
                force[a, ma] = force[b, mb] = None
                both = (mode(a, ma) + mode(b, mb)) * stiff(4)
                force[a, ma] = force[b, mb] = both
                force[c, 7] = mode(c, 7) * stiff(5)
            x, y, z = (mode(0, 6), mode(1, 5), mode(2, 3))
            shared = (x + y + z) * stiff(7)
            force[0, 6] = x * stiff(6) + shared
            force[1, 5] = y * stiff(6) + shared
            force[2, 3] = z * stiff(6) + shared
            for a in range(3):
                for m in range(4):
                    high = force[a, m + 4]
                    low = force.get((a, m))
                    if e >= 1:
                        add((e - 1, a, m), -high if low is None else low - high)
                    if e <= 1:
                        add((e, a, m), high if low is None else low + high)
            below = above
        for l in range(2):
            for a in range(3):
                g = [acc[l, a, m] for m in range(4)]
                total = (g[0] - g[1]) + pltpu.roll(g[0] + g[1], 1, axis=0)
                slope = (g[2] - g[3]) + pltpu.roll(g[2] + g[3], 1, axis=0)
                partial[l, a, h] = (total - slope, total + slope)
    result = {}
    for l in range(2):
        for a in range(3):
            moved = prior_along_y(partial[l, a, 0][1], partial[l, a, 1][1], lane)
            result[l, a] = jnp.concatenate(
                [partial[l, a, 0][0] + moved[0], partial[l, a, 1][0] + moved[1]], axis=1
            )
    return result


def split_bf16(value, parts):
    out = []
    for _ in range(parts):
        piece = value.astype(jnp.bfloat16)
        out.append(piece)
        value = value - piece.astype(f32)
    return out


def exact_dot(value, ones):
    rows = value.shape[0]
    parts = jnp.dot(jnp.concatenate(split_bf16(value, 3), axis=0), ones, preferred_element_type=f32)
    return (parts[2 * rows :] + parts[rows : 2 * rows]) + parts[:rows]


def exchange(
    slabs, cols, constants, rows_total,
    u_hbm, dens_hbm, solid_hbm, fixed_hbm,
    u_all, im_all, rows_ref,
    halo, dens, solid, fixed, scaled, gram_a, gram_b,
    local_sem, halo_send, halo_recv, u_send, u_recv, q_send, q_recv, im_send, im_recv, gram_send, gram_recv,
    ready_x, ready_z,
):
    s = lax.axis_index("slab")
    c = lax.axis_index("col")
    zn = slabs // 8
    zi = lax.div(s, 8)
    yc = s - 8 * zi
    yi = lax.div(yc, 2)
    core = yc - 2 * yi
    plane, depth2 = (cols * 8, zn)

    def wrap(value, k, count):
        moved = value + k % count
        return jnp.where(moved >= count, moved - count, moved)

    def at(slab, col):
        return {"slab": slab, "col": col}

    def along_x(k):
        return at(s, wrap(c, k, cols))

    def along_z(k, m=0):
        return at(wrap(zi, k, zn) * 8 + 2 * yi + (1 - core if m else core), c)

    up, down = (at(wrap(s, 1, slabs), c), at(wrap(s, -1, slabs), c))
    near = [up, down] + [along_z(k) for k in (1, -1)]
    near += [along_x(k) for k in range(1, cols)]
    near += [at(8 * zi + wrap(yc, k, 8), c) for k in range(1, 8)]

    local = [
        pltpu.make_async_copy(u_hbm, u_all.at[c], local_sem.at[0]),
        pltpu.make_async_copy(dens_hbm, dens.at[pl.ds(1, 2)], local_sem.at[1]),
        pltpu.make_async_copy(solid_hbm, solid.at[pl.ds(1, 2)], local_sem.at[2]),
        pltpu.make_async_copy(fixed_hbm, fixed.at[pl.ds(1, 2)], local_sem.at[3]),
    ]
    barrier = pltpu.get_barrier_semaphore()
    for partner in near:
        pl.semaphore_signal(barrier, inc=1, device_id=partner, device_id_type=MESH)
    for copy in local:
        copy.start()
    for copy in local:
        copy.wait()
    pl.semaphore_wait(barrier, len(near))

    def remote(src, dst, send, recv, where):
        return pltpu.make_async_remote_copy(
            src_ref=src, dst_ref=dst, send_sem=send, recv_sem=recv, device_id=where, device_id_type=MESH
        )

    def received(ref, sem):
        remote(ref, ref, sem, sem, along_x(1)).wait_recv()

    def sent(ref, sem):
        remote(ref, ref, sem, sem, along_x(1)).wait_send()

    small_send, small_recv = (halo_send.at[4], halo_recv.at[4])
    remote(dens.at[2], dens.at[0], small_send, small_recv, up).start()
    remote(solid.at[2], solid.at[0], small_send, small_recv, up).start()
    remote(fixed.at[2], fixed.at[0], small_send, small_recv, up).start()
    remote(fixed.at[1], fixed.at[3], small_send, small_recv, down).start()
    for j in range(4):
        remote(u_all.at[c, j, :, 1], halo.at[0, j], halo_send.at[j], halo_recv.at[j], up).start()
        remote(u_all.at[c, j, :, 0], halo.at[1, j], halo_send.at[j], halo_recv.at[j], down).start()

    first_pair, last_pair = (pl.ds(0, 2), pl.ds(2, 2))
    def share(part):
        ref = u_all.at[c, part]
        pl.when(c < cols - 1)(remote(ref, ref, u_send.at[0], u_recv.at[0], along_x(1)).start)
        pl.when(c == 0)(remote(ref, ref, u_send.at[1], u_recv.at[1], along_x(-1)).start)

    share(pl.ds(0, 3))

    for k in range(1, cols):
        pl.semaphore_signal(ready_x, inc=1, device_id=along_x(k), device_id_type=MESH)
    for k in (1, -1):
        pl.semaphore_signal(ready_z.at[0], inc=1, device_id=along_z(k), device_id_type=MESH)

    received(fixed, small_recv)

    node = lax.broadcasted_iota(jnp.int32, (8, 256), 0)
    along = lax.broadcasted_iota(jnp.int32, (8, 256), 1)
    inside = (node < 7) & (along < 255)
    for e in range(3):
        depth = s * 2 - 1 + e
        value = solid[e].astype(f32) * (dens[e] * dens[e] * dens[e]) + void_stiffness
        keep = inside & (depth >= 0) & (depth < 2 * slabs - 1)
        value = jnp.where(keep, value, 0.0)
        for k, constant in enumerate(constants):
            scaled[e, k] = value * constant

    lane = lax.broadcasted_iota(jnp.int32, (8, 128), 1)

    def halves(t):
        layer = jnp.where(t >= 2, 1, 0)
        return (layer, t - 2 * layer)

    def one_column(j, carry):
        free = [1.0 - fixed[l].astype(f32) for l in range(4)]
        raw = [[u_all[c, j, a, l] for a in range(3)] for l in range(2)]
        received(halo.at[:, 0], halo_recv.at[j])
        layers = [
            [halo[0, j, a] * free[0] for a in range(3)],
            [raw[0][a] * free[1] for a in range(3)],
            [raw[1][a] * free[2] for a in range(3)],
            [halo[1, j, a] * free[3] for a in range(3)],
        ]
        out = column_image(layers, scaled, lane)
        for l in range(2):
            for a in range(3):
                value = free[l + 1] * out[l, a] + (1.0 - free[l + 1]) * raw[l][a]
                im_all[c, j, a, l, 0] = value[:, :128]
                im_all[c, j, a, l, 1] = value[:, 128:]
        for k in (2, 1, 3):
            t = wrap(c, k, cols)
            piece = im_all.at[c, j, :, *halves(t)]
            remote(piece, piece, q_send, q_recv, at(s, t)).start()
        return carry

    lax.fori_loop(0, 4, one_column, 0)

    share(pl.ds(3, 1))
    u_back = remote(u_all.at[c, last_pair], u_all.at[c, last_pair], u_send.at[2], u_recv.at[2], along_x(-1))
    pl.when(c == 1)(u_back.start)

    pl.semaphore_wait(ready_z.at[0], 2)
    for k in (2, -2):
        pl.semaphore_signal(ready_z.at[1], inc=1, device_id=along_z(k), device_id_type=MESH)
    pl.semaphore_wait(ready_x, cols - 1)

    quarters = im_all.at[pl.ds(0, cols - 1), :, :, 0, 0]
    received(quarters, q_recv)

    mine_l, mine_h = halves(c)
    sides = []
    for a in range(3):
        block = im_all[:, :, a, mine_l, mine_h].reshape(128, 128)
        sides.append(jnp.concatenate(split_bf16(block, 2), axis=0))
    total = None
    for both in (jnp.concatenate(sides[:2], axis=1), sides[2]):
        part = lax.dot_general(both, both, (((1,), (1,)), ((), ())), preferred_element_type=f32)
        total = part if total is None else total + part
    pairs = (total[:128, :128] + total[128:, 128:]) + (total[:128, 128:] + total[128:, :128])
    row_id = lax.broadcasted_iota(jnp.int32, (128, 128), 0)
    col_id = lax.broadcasted_iota(jnp.int32, (128, 128), 1)
    pairs = jnp.where(row_id % 8 == col_id % 8, pairs, 0.0).reshape(16, 8, 128).sum(axis=1)
    row16 = lax.broadcasted_iota(jnp.int32, (16, 128), 0)
    lane16 = lax.broadcasted_iota(jnp.int32, (16, 128), 1)
    spread = (row_id // 8 == col_id // 8).astype(jnp.bfloat16)
    pairs = exact_dot(pairs, spread)
    packed = jnp.where(row16 % 8 == lane16 % 8, pairs, 0.0).reshape(2, 8, 128).sum(axis=1)

    slot = 8 * c + yc
    gram_a[slot] = packed
    hops = [(min(k, cols - k) + min(m // 2, 4 - m // 2), k, m) for k in range(cols) for m in range(8)]
    for _, k, m in sorted(hops, reverse=True)[:-1]:
        where = at(8 * zi + wrap(yc, m, 8), wrap(c, k, cols))
        remote(gram_a.at[slot], gram_a.at[slot], gram_send.at[0], gram_recv.at[0], where).start()

    for k in range(1, cols):
        piece = im_all.at[c, :, :, *halves(wrap(c, 1 + k, cols))]
        pl.when(c < cols - 1)(remote(piece, piece, im_send.at[0], im_recv.at[0], along_x(1)).start)
        piece = im_all.at[c, :, :, (k - 1) // 2, (k - 1) % 2]
        pl.when(c == 0)(remote(piece, piece, im_send.at[1], im_recv.at[1], along_x(-1)).start)
    piece = im_all.at[c, :, :, 1, 0]
    im_back = remote(piece, piece, im_send.at[2], im_recv.at[2], along_x(-1))
    pl.when(c == 1)(im_back.start)

    ahead = (c == 1) | (c == 2)
    relay_block = jnp.where(ahead, c - 1, wrap(c, 1, cols))
    pl.when(c >= 1)(lambda: received(u_all.at[0], u_recv.at[0]))
    pl.when(c == 3)(lambda: received(u_all.at[0], u_recv.at[1]))
    pl.when(c == 0)(lambda: received(u_all.at[0, last_pair], u_recv.at[2]))
    ref = u_all.at[relay_block, first_pair]
    pl.when(ahead)(remote(ref, ref, u_send.at[3], u_recv.at[3], along_x(1)).start)
    ref = u_all.at[relay_block, last_pair]
    pl.when(jnp.logical_not(ahead))(remote(ref, ref, u_send.at[4], u_recv.at[4], along_x(-1)).start)

    pl.semaphore_wait(ready_z.at[1], 2)
    received(gram_a.at[pl.ds(0, plane - 1)], gram_recv.at[0])
    gram_b[zi] = jnp.sum(gram_a[...], axis=0)
    for k in sorted(range(1, zn), key=lambda k: -min(k, zn - k)):
        remote(gram_b.at[zi], gram_b.at[zi], gram_send.at[1], gram_recv.at[1], along_z(k)).start()

    pl.when(c >= 1)(lambda: received(quarters, im_recv.at[0]))
    pl.when(c == 3)(lambda: received(quarters, im_recv.at[1]))
    pl.when(c == 0)(lambda: received(im_all.at[0, :, :, 0, 0], im_recv.at[2]))
    ref = im_all.at[relay_block, :, :, 0]
    pl.when(ahead)(remote(ref, ref, im_send.at[3], im_recv.at[3], along_x(1)).start)
    ref = im_all.at[relay_block, :, :, 1, jnp.where(c == 3, 1, 0)]
    pl.when(jnp.logical_not(ahead))(remote(ref, ref, im_send.at[4], im_recv.at[4], along_x(-1)).start)

    received(gram_b.at[pl.ds(0, depth2 - 1)], gram_recv.at[1])
    summed = jnp.sum(gram_b[...], axis=0)

    wide_rows = jnp.concatenate([jnp.broadcast_to(summed[r : r + 1], (8, 128)) for r in range(2)], axis=0)
    kept = jnp.where(row16 % 8 == lane16 % 8, wide_rows, 0.0)
    picked = (row_id // 8 == col_id).astype(jnp.bfloat16)
    gram = exact_dot(kept, picked) * (1.0 / rows_total)

    work = jnp.where(lane16 < 16, gram, (lane16 == row16 + 16).astype(f32))
    for first in range(0, 16, 4):
        ids = range(4)
        side = [jnp.broadcast_to(work[:, first + b : first + b + 1], (16, 128)) for b in ids]
        rows = [work[first + a : first + a + 1] for a in ids]
        low = {}
        scale = []
        for b in ids:
            for a in range(b, 4):
                value = side[b][first + a : first + a + 1]
                for d in range(b):
                    value = value - low[a, d] * low[b, d]
                if a == b:
                    scale.append(lax.rsqrt(value))
                else:
                    low[a, b] = value * scale[b]
        for b in ids:
            for d in range(b):
                rows[b] = rows[b] - low[b, d] * rows[d]
                side[b] = side[b] - side[d] * low[b, d]
            rows[b] = rows[b] * scale[b]
            side[b] = side[b] * scale[b]
            rows_ref[first + b : first + b + 1, :] = rows[b]
        if first < 12:
            work = work - ((side[0] * rows[0] + side[1] * rows[1]) + (side[2] * rows[2] + side[3] * rows[3]))

    pl.when((c == 2) | (c == 3))(lambda: received(u_all.at[0, first_pair], u_recv.at[3]))
    pl.when((c == 2) | (c == 3))(lambda: received(u_all.at[0, first_pair], u_recv.at[4]))
    pl.when((c == 2) | (c == 3))(lambda: received(im_all.at[0, :, :, 0], im_recv.at[3]))
    pl.when((c == 2) | (c == 3))(lambda: received(im_all.at[0, :, :, 0, 0], im_recv.at[4]))
    sent(fixed, small_send)
    for j in range(4):
        sent(halo.at[:, 0], halo_send.at[j])
    sent(quarters, q_send)
    sent(gram_a.at[pl.ds(0, plane - 1)], gram_send.at[0])
    sent(gram_b.at[pl.ds(0, depth2 - 1)], gram_send.at[1])
    pl.when(c < cols - 1)(lambda: sent(u_all.at[0], u_send.at[0]))
    pl.when(c == 0)(lambda: sent(u_all.at[0], u_send.at[1]))
    pl.when(c == 1)(lambda: sent(u_all.at[0, first_pair], u_send.at[2]))
    pl.when(c < cols - 1)(lambda: sent(quarters, im_send.at[0]))
    pl.when(c == 0)(lambda: sent(quarters, im_send.at[1]))
    pl.when(c == 1)(lambda: sent(im_all.at[0, :, :, 0, 0], im_send.at[2]))
    pl.when(ahead)(lambda: sent(u_all.at[0, first_pair], u_send.at[3]))
    pl.when(ahead)(lambda: sent(im_all.at[0, :, :, 0], im_send.at[3]))
    pl.when(jnp.logical_not(ahead))(lambda: sent(u_all.at[0, first_pair], u_send.at[4]))
    pl.when(jnp.logical_not(ahead))(lambda: sent(im_all.at[0, :, :, 0, 0], im_send.at[4]))


def combine(u_all, im_all, rows_ref, ortho_hbm, renew_hbm, r_hbm, ortho, renew, r_ref, coef_ref, out_sem):
    c = lax.axis_index("col")
    row16 = lax.broadcasted_iota(jnp.int32, (16, 128), 0)
    lane16 = lax.broadcasted_iota(jnp.int32, (16, 128), 1)
    r_ref[...] = jnp.where(lane16 >= row16, rows_ref[...], 0.0)[:, :16]
    factor_out = pltpu.make_async_copy(r_ref, r_hbm, out_sem.at[2])
    own = rows_ref[pl.ds(4 * c, 4), :]
    for j in range(16):
        coef_ref[j] = jnp.broadcast_to(own[:, 16 + j : 17 + j], (4, 128))

    def used(j, value):
        return value if j < 4 else jnp.where(j // 4 <= c, value, 0.0)

    def outputs(step):
        a, l = step // 2, step % 2
        return [
            pltpu.make_async_copy(ortho.at[:, a, l], ortho_hbm.at[:, a, l], out_sem.at[0]),
            pltpu.make_async_copy(renew.at[:, a, l], renew_hbm.at[:, a, l], out_sem.at[1]),
        ]

    def one(step, carry):
        a, l = step // 2, step % 2
        for h in range(2):
            for source, target in ((u_all, renew), (im_all, ortho)):
                acc = [None] * 4
                for j in range(16):
                    if source is u_all:
                        value = source[j // 4, j % 4, a, l, :, 128 * h : 128 * h + 128]
                    else:
                        value = source[j // 4, j % 4, a, l, h]
                    value = used(j, value)
                    for i in range(4):
                        term = coef_ref[j, i : i + 1, :] * value
                        acc[i] = term if acc[i] is None else acc[i] + term
                for i in range(4):
                    target[i, a, l, :, 128 * h : 128 * h + 128] = acc[i]
        for copy in outputs(step):
            copy.start()
        return carry

    factor_out.start()
    lax.fori_loop(0, 6, one, 0)
    pltpu.make_async_copy(ortho, ortho_hbm, out_sem.at[0]).wait()
    pltpu.make_async_copy(renew, renew_hbm, out_sem.at[1]).wait()
    factor_out.wait()


def solution(mesh):
    slabs, cols = (mesh.shape["slab"], mesh.shape["col"])
    constants = mode_constants()

    def on_device(recycle_basis, densities, solid_mask, fixed_mask):
        shape = recycle_basis.shape
        rows_total = 3 * slabs * shape[2] * shape[3] * shape[4]
        vmem = pl.BlockSpec(memory_space=pltpu.VMEM)
        hbm = pl.BlockSpec(memory_space=pl.ANY)
        dma = pltpu.SemaphoreType.DMA
        layer = shape[3:]
        u_all, im_all, rows = pl.pallas_call(
            functools.partial(exchange, slabs, cols, constants, float(rows_total)),
            out_shape=(
                pltpu.VMEM((cols,) + shape, f32),
                pltpu.VMEM((cols,) + shape[:3] + (2, 8, 128), f32),
                pltpu.VMEM((16, 128), f32),
            ),
            in_specs=[hbm] * 4,
            out_specs=(vmem, vmem, vmem),
            scratch_shapes=[
                pltpu.VMEM((2, 4, 3) + layer, f32),
                pltpu.VMEM((3,) + layer, f32),
                pltpu.VMEM((3,) + layer, jnp.int32),
                pltpu.VMEM((4,) + layer, jnp.int32),
                pltpu.VMEM((3, len(constants)) + layer, f32),
                pltpu.VMEM((cols * 8, 2, 128), f32),
                pltpu.VMEM((slabs // 8, 2, 128), f32),
                dma((4,)), dma((5,)), dma((5,)), dma((5,)), dma((5,)),
                dma, dma, dma((5,)), dma((5,)), dma((2,)), dma((2,)),
                pltpu.SemaphoreType.REGULAR, pltpu.SemaphoreType.REGULAR((2,)),
            ],
            compiler_params=pltpu.CompilerParams(collective_id=0, has_side_effects=True),
        )(recycle_basis, densities, solid_mask, fixed_mask)
        kept = [pltpu.with_memory_space_constraint(x, pltpu.VMEM) for x in (u_all, im_all, rows)]
        return pl.pallas_call(
            combine,
            out_shape=(
                jax.ShapeDtypeStruct(shape, f32),
                jax.ShapeDtypeStruct(shape, f32),
                jax.ShapeDtypeStruct((16, 16), f32),
            ),
            in_specs=[vmem] * 3,
            out_specs=(hbm, hbm, hbm),
            scratch_shapes=[
                pltpu.VMEM(shape, f32),
                pltpu.VMEM(shape, f32),
                pltpu.VMEM((16, 16), f32),
                pltpu.VMEM((16, 4, 128), f32),
                dma((3,)),
            ],
        )(*kept)

    placed = (
        P("col", None, "slab", None, None),
        P("slab", None, None),
        P("slab", None, None),
        P("slab", None, None),
    )
    return jax.shard_map(
        on_device,
        mesh=mesh,
        in_specs=placed,
        out_specs=(P("col", None, "slab", None, None), P("col", None, "slab", None, None), P()),
        check_vma=False,
    )
```
